32 devices in a mesh: ctx: 8 (over y, x, core), kvh: 4 (over z).
Axes of the slice: x: 2, y: 2, z: 4, core: 2. Of those that a mesh axis runs over, the one named last changes fastest.
Arguments:
- queries: bfloat16 [3072, 32, 128], P('ctx', 'kvh'), may hold values from -320 to 320
- keys: bfloat16 [3072, 4, 128], P('ctx', 'kvh'), may hold values from -6 to 6
- values: bfloat16 [3072, 4, 128], P('ctx', 'kvh'), may hold values from -6 to 6
- vert_blocks: int32 [4, 16], P('kvh'), may hold values from 0 to 47, as said below
- slash_offsets: int32 [4, 8], P('kvh'), may hold values from 1 to 24, as said below
- out_weight: bfloat16 [4096, 4, 1024], P('ctx', 'kvh'), may hold values from -0.09375 to 0.09375
Outputs:
- mixed: bfloat16 [3072, 4096], P('ctx', 'kvh')
The draws below stay inside these ranges and needn't reach their ends.
Inputs may be any that keep to these rules, and one draw needn't show every extreme that they name: `vert_blocks`: within each KV head the 16 block indices are distinct; some head lists block 0 and block 47. `slash_offsets`: within each KV head the 8 offsets are distinct; some head has offset 1 and offset 24.
All inputs are finite; a program needn't handle non-finite values.
Results may differ from the reference program's by a relative error of at most 0.017.
Values may be sent and summed in bfloat16 or wider, within the bound.
A program may use at most 128 MiB of HBM per device.

```python
import math
import jax
import jax.numpy as jnp
from jax import lax

HD = 128
GROUP = 8
KVH = 4
QH = 32
D_OUT = 4096
BLK = 64
SPAN = 4
TOK_DEV = 384
VERT = 16
SLASH = 8
TOKENS = 3072
REACH = 24
N_CTX = 8
N_KVH = 4


def draw_queries(key, part):
    base = jax.random.truncated_normal(key, -8.0, 8.0, (TOKENS, QH, HD), jnp.float32)
    return base.astype(jnp.bfloat16)


def draw_vert_blocks(key, part):
    block_count = TOKENS // BLK
    first_head = jnp.concatenate([jnp.array([block_count - 1, 0], jnp.int32), (jax.random.permutation(jax.random.fold_in(key, 101), block_count - 2)[:VERT - 2] + 1).astype(jnp.int32)])
    listed = [first_head]
    for head_id in range(1, KVH):
        listed.append(jax.random.permutation(jax.random.fold_in(key, 101 + head_id), block_count)[:VERT].astype(jnp.int32))
    return jnp.stack(listed)


def draw_slash_offsets(key, part):
    first_head = jnp.concatenate([jnp.array([REACH, 1], jnp.int32), (jax.random.permutation(jax.random.fold_in(key, 201), REACH - 2)[:SLASH - 2] + 2).astype(jnp.int32)])
    listed = [first_head]
    for head_id in range(1, KVH):
        listed.append((jax.random.permutation(jax.random.fold_in(key, 201 + head_id), REACH)[:SLASH] + 1).astype(jnp.int32))
    return jnp.stack(listed)


def block_levels(own_key, shape, shards, smallest, top_value):
    def one(position, shards_of):
        heights = jax.random.uniform(jax.random.fold_in(jax.random.fold_in(own_key, 6), position), (shards_of,), jnp.float32, smallest / len(shards), top_value / len(shards))
        return jnp.repeat(jnp.exp(heights), shape[position] // shards_of).reshape((-1,) + (1,) * (len(shape) - position - 1))

    factor_of = one(*shards[0])
    for cut in shards[1:]:
        factor_of = factor_of * one(*cut)
    return factor_of


def scatter_about(own_key, dims, deviation, most, cuts=(), kind=jnp.bfloat16):
    values = deviation * jax.random.normal(own_key, dims, jnp.float32)
    if cuts:
        values = values * block_levels(own_key, dims, cuts, -0.22, 0.18)
    return jnp.clip(values, -most, most).astype(kind)


def setup_inputs(seed: int = 0) -> dict:
    key_of = jax.random.split(jax.random.key(seed), 7)
    queries = draw_queries(jax.random.fold_in(key_of[6], 71), 0)
    keys = scatter_about(key_of[1], (TOKENS, KVH, HD), 1.0, 6.0, ((0, 8), (1, 4)))
    values = scatter_about(key_of[2], (TOKENS, KVH, HD), 1.0, 6.0, ((0, 8), (1, 4)))
    vert_blocks = draw_vert_blocks(jax.random.fold_in(key_of[6], 71), 0)
    slash_offsets = draw_slash_offsets(jax.random.fold_in(key_of[6], 71), 0)
    out_weight = scatter_about(key_of[5], (QH * HD, N_KVH, D_OUT // N_KVH), (QH * HD) ** -0.5, 0.09375, ((0, 8), (1, 4)))
    return dict(queries=queries, keys=keys, values=values, vert_blocks=vert_blocks, slash_offsets=slash_offsets, out_weight=out_weight)


NEG_FILL = -1e+30

def reference(queries, keys, values, vert_blocks, slash_offsets, out_weight):
    score_scale = 1.0 / math.sqrt(HD)
    front_pad = SPAN * TOK_DEV
    window_len = (SPAN + 1) * TOK_DEV
    key_pad = jnp.concatenate([jnp.zeros((front_pad, KVH, HD), keys.dtype), keys], axis=0)
    value_pad = jnp.concatenate([jnp.zeros((front_pad, KVH, HD), values.dtype), values], axis=0)
    head_ids = jnp.arange(KVH, dtype=jnp.int32)[:, None]
    vert_pos = (vert_blocks[:, :, None] * BLK + jnp.arange(BLK, dtype=jnp.int32)[None, None, :]).reshape(KVH, VERT * BLK)
    vert_keys = keys[vert_pos, head_ids].astype(jnp.float32)
    vert_values = values[vert_pos, head_ids].astype(jnp.float32)
    vert_block_ids = vert_pos // BLK
    out_matrix = out_weight.reshape(QH * HD, D_OUT)

    def one_range(device_id):
        range_start = (device_id * TOK_DEV).astype(jnp.int32)
        query_pos = range_start + jnp.arange(TOK_DEV, dtype=jnp.int32)
        key_pos = range_start - front_pad + jnp.arange(window_len, dtype=jnp.int32)
        query_rows = lax.dynamic_slice_in_dim(queries, range_start, TOK_DEV, 0).reshape(TOK_DEV, KVH, GROUP, HD).astype(jnp.float32)
        key_window = lax.dynamic_slice_in_dim(key_pad, range_start, window_len, 0).astype(jnp.float32)
        value_window = lax.dynamic_slice_in_dim(value_pad, range_start, window_len, 0).astype(jnp.float32)
        window_diff = query_pos[:, None] // BLK - key_pos[None, :] // BLK
        window_hits = jnp.any(window_diff[None, :, :, None] == slash_offsets[:, None, None, :], axis=-1)
        window_keep = (key_pos[None, :] <= query_pos[:, None]) & (key_pos[None, :] >= 0)
        window_keep = window_keep[None] & ((window_diff == 0)[None] | window_hits)
        vert_diff = query_pos[None, :, None] // BLK - vert_block_ids[:, None, :]
        vert_hits = jnp.any(vert_diff[..., None] == slash_offsets[:, None, None, :], axis=-1)
        vert_keep = (vert_diff > 0) & jnp.logical_not(vert_hits)
        window_score = jnp.einsum('thgd,shd->hgts', query_rows, key_window) * score_scale
        vert_score = jnp.einsum('thgd,hsd->hgts', query_rows, vert_keys) * score_scale
        window_score = jnp.where(window_keep[:, None], window_score, NEG_FILL)
        vert_score = jnp.where(vert_keep[:, None], vert_score, NEG_FILL)
        row_max = jnp.maximum(lax.optimization_barrier(jnp.max(window_score, axis=-1)), lax.optimization_barrier(jnp.max(vert_score, axis=-1)))
        window_weight = jnp.where(window_keep[:, None], jnp.exp(window_score - row_max[..., None]), 0.0)
        vert_weight = jnp.where(vert_keep[:, None], jnp.exp(vert_score - row_max[..., None]), 0.0)
        row_total = lax.optimization_barrier(jnp.sum(window_weight, axis=-1)) + lax.optimization_barrier(jnp.sum(vert_weight, axis=-1))
        window_round = lax.optimization_barrier(window_weight.astype(jnp.bfloat16)).astype(jnp.float32)
        vert_round = lax.optimization_barrier(vert_weight.astype(jnp.bfloat16)).astype(jnp.float32)
        weighted = jnp.einsum('hgts,shd->hgtd', window_round, value_window)
        weighted = weighted + jnp.einsum('hgts,hsd->hgtd', vert_round, vert_values)
        attention = (weighted / row_total[..., None]).transpose(2, 0, 1, 3).reshape(TOK_DEV, QH * HD).astype(jnp.bfloat16)
        return jnp.dot(attention, out_matrix, preferred_element_type=jnp.float32).astype(jnp.bfloat16)
    projected = lax.map(one_range, jnp.arange(N_CTX, dtype=jnp.int32))
    return projected.reshape(TOKENS, D_OUT)
```

```python
import functools
import math

import jax
import jax.numpy as jnp
from jax import lax
from jax.experimental import pallas as pl
from jax.experimental.pallas import tpu as pltpu
from jax.sharding import PartitionSpec as P

BLK = 64
CORES = 2
NEG_FILL = -1e30
AGAIN = 2
EARLY = 3
AHEAD = 2
OUT_PARTS = 3


def kernel(
    n_ctx, n_kvh, n_slash, n_vert,
    vert_ref, slash_ref, q_ref, k_ref, v_ref, w_ref, out_ref,
    kv_buf, w_buf, att_buf, kg, vg, bias, q_raw, q_wide, q_buf, acc, out_buf,
    local_sem, kv_recv, kv_send, kv_fwd, w_recv, w_send, w_fwd, z_recv, z_up, z_down, out_sem,
):
    c = lax.axis_index("ctx")
    z = lax.axis_index("kvh")
    n_chip = n_ctx // CORES
    chip, core = c // CORES, c % CORES
    sibling = chip * CORES + (1 - core)
    blocks = k_ref.shape[0]
    tokens, heads, head_size = q_ref.shape
    kv_refs = (k_ref, v_ref)
    w_rows = w_ref.shape[0]
    n_slots = kg.shape[0] // BLK

    def peer(step):
        return lax.rem(chip + step, n_chip) * CORES + core

    def sibling_source(step):
        return lax.rem(chip + n_chip - step, n_chip) * CORES + (1 - core)

    def kv_at(part, owner):
        return kv_buf.at[part, pl.ds(owner * blocks, blocks)]

    half_rows = w_rows // 2

    def w_at(owner, half):
        first = pl.multiple_of(owner * w_rows + half * half_rows, half_rows)
        return w_buf.at[pl.ds(first, half_rows)]

    def own_rows(half):
        return w_ref.at[pl.ds(half * half_rows, half_rows)]

    def push(src, dst, send_sem, recv_sem, to_ctx, to_z):
        return pltpu.make_async_remote_copy(
            src_ref=src, dst_ref=dst, send_sem=send_sem, recv_sem=recv_sem,
            device_id=(to_ctx, to_z), device_id_type=pl.DeviceIdType.MESH,
        )

    own_q = pltpu.make_async_copy(q_ref, q_raw, local_sem.at[2])
    own_q.start()
    own_w = [
        pltpu.make_async_copy(own_rows(half), w_at(c, half), local_sem.at[3 + half])
        for half in (0, 1)
    ]

    barrier = pltpu.get_barrier_semaphore()

    def greet(to_ctx, to_z):
        pl.semaphore_signal(
            barrier, inc=1, device_id=(to_ctx, to_z), device_id_type=pl.DeviceIdType.MESH
        )

    @pl.loop(1, n_chip)
    def _(step):
        greet(peer(step), z)

    greet(sibling, z)

    @pl.when(z > 0)
    def _():
        greet(c, z - 1)

    @pl.when(z < n_kvh - 1)
    def _():
        greet(c, z + 1)

    inner = jnp.where(z > 0, 1, 0) + jnp.where(z < n_kvh - 1, 1, 0)
    lane = lax.broadcasted_iota(jnp.int32, (BLK, 2 * BLK), 1)
    row = lax.broadcasted_iota(jnp.int32, (BLK, 2 * BLK), 0)

    @pl.loop(0, blocks)
    def _(block):
        place = c * blocks + block
        fills = [jnp.float32(0.0)]
        for j in range(n_slash):
            fills.append(jnp.where(place - slash_ref[0, j] >= 0, 0.0, NEG_FILL))
        for j in range(n_vert):
            gap = place - vert_ref[0, j]
            fill = jnp.where(gap > 0, 0.0, NEG_FILL)
            for k in range(n_slash):
                fill = jnp.where(gap == slash_ref[0, k], NEG_FILL, fill)
            fills.append(fill)
        while len(fills) < n_slots:
            fills.append(jnp.float32(NEG_FILL))
        for j in range(0, n_slots, 2):
            fill = jnp.where(lane < BLK, fills[j], fills[j + 1])
            if j == 0:
                fill = jnp.where((lane < BLK) & (lane > row), NEG_FILL, fill)
            bias[block, :, j * BLK:(j + 2) * BLK] = fill

    pl.semaphore_wait(barrier, n_chip + inner)

    square = n_chip == 4
    beside = (chip // 2) * 2 + (1 - chip % 2)
    behind = (1 - chip // 2) * 2 + chip % 2
    corner = n_chip - 1 - chip

    own_kv = [
        pltpu.make_async_copy(kv_refs[part], kv_at(part, c), local_sem.at[part]) for part in (0, 1)
    ]

    def kv_direct(to_chip, part, slot):
        return push(
            kv_refs[part], kv_at(part, c), kv_send.at[part, slot], kv_recv.at[part, c],
            to_chip * CORES + core, z,
        )

    def kv_arrival(owner, part):
        rows = kv_at(part, owner)
        return push(rows, rows, kv_send.at[part, 0], kv_recv.at[part, owner], c, z)

    def kv_across(owner, part, slot):
        rows = kv_at(part, owner)
        return push(rows, rows, kv_fwd.at[part, slot], kv_recv.at[part, owner], sibling, z)

    def kv_corner(part):
        from_chip, to_chip = (beside, behind) if part == 0 else (behind, beside)
        owner = from_chip * CORES + core
        rows = kv_at(part, owner)
        return push(
            rows, rows, kv_send.at[part, 0], kv_recv.at[part, owner], to_chip * CORES + core, z
        )

    def kv_pass(chip_from, part, slot):
        owner = chip_from * CORES + core
        kv_arrival(owner, part).wait_recv()
        kv_across(owner, part, slot).start()

    own_across = [
        push(kv_refs[part], kv_at(part, c), kv_fwd.at[part, 0], kv_recv.at[part, c], sibling, z)
        for part in (0, 1)
    ]

    if square:
        for first in (0, 1):
            kv_direct(beside, first, 1).start()
            kv_direct(behind, 1 - first, 2).start()
    else:

        @pl.loop(1, n_chip)
        def _(step):
            for part in (0, 1):
                kv_direct(lax.rem(chip + step, n_chip), part, step).start()

    for part in (0, 1):
        own_across[part].start()
        own_kv[part].start()

    for part in (0, 1):
        own_kv[part].wait()

    if square:
        for part, chip_from, slot in ((0, beside, 1), (1, behind, 2)):
            kv_arrival(chip_from * CORES + core, part).wait_recv()
            kv_corner(part).start()
            kv_across(chip_from * CORES + core, part, slot).start()

    own_q.wait()

    @pl.loop(0, blocks)
    def _(block):
        first_row = pl.multiple_of(block * BLK, BLK)
        wide = q_raw[pl.ds(first_row, BLK)].astype(jnp.float32)
        q_wide[...] = wide.reshape(BLK * heads, head_size)
        for h in range(heads):
            q_buf[h, pl.ds(first_row, BLK), :] = q_wide[
                pl.ds(h, BLK, stride=heads), :
            ].astype(jnp.bfloat16)

    if square:
        kv_pass(beside, 1, 1)
        kv_pass(behind, 0, 2)
        for part in (0, 1):
            kv_pass(corner, part, 3)
    else:

        @pl.loop(1, n_chip)
        def _(step):
            for part in (0, 1):
                kv_pass(lax.rem(chip + step, n_chip), part, step)

    def w_direct(to_chip, half, slot):
        return push(
            own_rows(half), w_at(c, half), w_send.at[slot, half], w_recv.at[c, half],
            to_chip * CORES + core, z,
        )

    def w_arrival(owner, half):
        return push(
            w_at(owner, half), w_at(owner, half), w_send.at[0, half], w_recv.at[owner, half], c, z
        )

    def w_across(owner, half, slot):
        return push(
            w_at(owner, half), w_at(owner, half), w_fwd.at[slot, half], w_recv.at[owner, half],
            sibling, z,
        )

    def w_corner(half):
        from_chip, to_chip = (beside, behind) if half == 0 else (behind, beside)
        owner = from_chip * CORES + core
        return push(
            w_at(owner, half), w_at(owner, half), w_send.at[0, half], w_recv.at[owner, half],
            to_chip * CORES + core, z,
        )

    if square:
        for first in (0, 1):
            w_direct(beside, first, 1).start()
            w_direct(behind, 1 - first, 2).start()
    else:

        @pl.loop(1, n_chip)
        def _(step):
            for half in (0, 1):
                w_direct(lax.rem(chip + step, n_chip), half, step).start()

    own_w_across = [
        push(own_rows(half), w_at(c, half), w_fwd.at[0, half], w_recv.at[c, half], sibling, z)
        for half in (0, 1)
    ]
    for half in (0, 1):
        own_w_across[half].start()
        own_w[half].start()

    def w_pass(chip_from, half, slot):
        owner = chip_from * CORES + core
        w_arrival(owner, half).wait_recv()
        w_across(owner, half, slot).start()

    @pl.loop(0, n_chip)
    def _(step):
        for part in (0, 1):
            kv_arrival(sibling_source(step), part).wait_recv()

    def z_copy(owner, block, sems, to_z):
        rows = att_buf.at[owner, pl.ds(pl.multiple_of(block * BLK, BLK), BLK)]
        return push(rows, rows, sems.at[owner, block], z_recv.at[owner, block], c, to_z)

    exponent_scale = math.log2(math.e) / math.sqrt(head_size)

    @pl.loop(0, blocks)
    def _(block):
        place = c * blocks + block
        picks = [place] + [jnp.maximum(place - slash_ref[0, j], 0) for j in range(n_slash)]
        picks += [vert_ref[0, j] for j in range(n_vert)]
        picks += [place] * (n_slots - len(picks))
        for j, pick in enumerate(picks):
            kg[j * BLK:(j + 1) * BLK, :] = kv_buf[0, pick]
            vg[j * BLK:(j + 1) * BLK, :] = kv_buf[1, pick]

        first_row = pl.multiple_of(block * BLK, BLK)
        part = heads // 2
        for half in range(2):
            rows = q_buf[half * part:(half + 1) * part, pl.ds(first_row, BLK), :]
            scores = lax.dot_general(
                rows.reshape(part * BLK, head_size), kg[...], (((1,), (1,)), ((), ())),
                preferred_element_type=jnp.float32,
            )
            scores = scores.reshape(part, BLK, n_slots * BLK) + bias[block][None]
            scores = scores.reshape(part * BLK, n_slots * BLK)
            peak = jnp.max(scores, axis=-1, keepdims=True)
            weights = jnp.exp2((scores - peak) * exponent_scale)
            total = jnp.sum(weights, axis=-1, keepdims=True)
            mixed = jnp.dot(
                weights.astype(jnp.bfloat16), vg[...], preferred_element_type=jnp.float32
            )
            mixed = (mixed / total).astype(jnp.bfloat16)
            for h in range(part):
                col = (half * part + h) * head_size
                att_buf[z, pl.ds(first_row, BLK), col:col + head_size] = mixed[
                    h * BLK:(h + 1) * BLK
                ]

        @pl.when(z < n_kvh - 1)
        def _():
            z_copy(z, block, z_up, z + 1).start()

        @pl.when(z > 0)
        def _():
            z_copy(z, block, z_down, z - 1).start()

    def line_step(block, distance):
        @pl.when(z >= distance)
        def _():
            z_copy(z - distance, block, z_up, z).wait_recv()

            if distance < n_kvh - 1:
                @pl.when(z < n_kvh - 1)
                def _():
                    z_copy(z - distance, block, z_up, z + 1).start()

        @pl.when(z + distance < n_kvh)
        def _():
            z_copy(z + distance, block, z_down, z).wait_recv()

            if distance < n_kvh - 1:
                @pl.when(z > 0)
                def _():
                    z_copy(z + distance, block, z_down, z - 1).start()

    if square:
        for half, chip_from, slot in ((0, beside, 1), (1, behind, 2)):
            w_arrival(chip_from * CORES + core, half).wait_recv()
            w_corner(half).start()
            w_across(chip_from * CORES + core, half, slot).start()

    for distance in range(1, n_kvh - 1):

        @pl.loop(0, blocks)
        def _(block, distance=distance):
            line_step(block, distance)

        if square and distance == 1:
            w_pass(beside, 1, 1)
            w_pass(behind, 0, 2)

    if square:
        for half in (0, 1):
            w_pass(corner, half, 3)
    else:

        @pl.loop(1, n_chip)
        def _(step):
            for half in (0, 1):
                w_pass(lax.rem(chip + step, n_chip), half, step)

    @pl.loop(0, n_chip)
    def _(step):
        for half in (0, 1):
            w_arrival(sibling_source(step), half).wait_recv()

    for half in (0, 1):
        own_w[half].wait()

    depth = att_buf.shape[2]
    tile = 256
    n_tiles = out_ref.shape[1] // tile
    parts = 2
    part_rows = tokens // parts
    part_blocks = blocks // parts

    def out_copy(p):
        rows = pl.ds(pl.multiple_of(p * part_rows, part_rows), part_rows)
        return pltpu.make_async_copy(out_buf.at[rows], out_ref.at[rows], out_sem.at[p])

    def product(owner, rows, cols):
        return jnp.dot(
            att_buf[owner, rows, :],
            w_buf[pl.ds(pl.multiple_of(owner * depth, depth), depth), cols],
            preferred_element_type=jnp.float32,
        )

    def add_product(owner):
        @pl.loop(0, n_tiles)
        def _(j):
            cols = pl.ds(pl.multiple_of(j * tile, tile), tile)
            acc[:, cols] += product(owner, slice(None), cols)

    @pl.loop(0, n_tiles)
    def _(j):
        cols = pl.ds(pl.multiple_of(j * tile, tile), tile)
        acc[:, cols] = product(z, slice(None), cols)

    for distance in range(1, n_kvh - 1):

        @pl.when(z >= distance)
        def _(distance=distance):
            add_product(z - distance)

        @pl.when(z + distance < n_kvh)
        def _(distance=distance):
            add_product(z + distance)

    last = n_kvh - 1
    at_end = (z == 0) | (z == last)
    far = last - z

    @pl.when(at_end)
    def _():
        @pl.loop(0, parts)
        def _(p):
            @pl.loop(0, part_blocks)
            def _(b):
                line_step(p * part_blocks + b, last)

            rows = pl.ds(pl.multiple_of(p * part_rows, part_rows), part_rows)

            @pl.loop(0, n_tiles)
            def _(j):
                cols = pl.ds(pl.multiple_of(j * tile, tile), tile)
                total = acc[rows, cols] + product(far, rows, cols)
                out_buf[rows, cols] = total.astype(out_ref.dtype)

            out_copy(p).start()

    @pl.when(jnp.logical_not(at_end))
    def _():
        out_buf[...] = acc[...].astype(out_ref.dtype)

        @pl.loop(0, parts)
        def _(p):
            out_copy(p).start()

    @pl.loop(0, parts)
    def _(p):
        out_copy(p).wait()

    for part in (0, 1):
        own_across[part].wait_send()
    for half in (0, 1):
        own_w_across[half].wait_send()

    @pl.loop(1, n_chip)
    def _(step):
        for part in (0, 1):
            kv_across(c, part, step).wait_send()
        for half in (0, 1):
            w_across(c, half, step).wait_send()

    if square:
        for half in (0, 1):
            w_corner(half).wait_send()
            w_direct(beside, half, 1).wait_send()
            w_direct(behind, half, 2).wait_send()
            kv_corner(half).wait_send()
            kv_direct(beside, half, 1).wait_send()
            kv_direct(behind, half, 2).wait_send()
    else:

        @pl.loop(1, n_chip)
        def _(step):
            for half in (0, 1):
                w_direct(lax.rem(chip + step, n_chip), half, step).wait_send()
                kv_direct(lax.rem(chip + step, n_chip), half, step).wait_send()

    for distance in range(n_kvh):

        @pl.loop(0, blocks)
        def _(block, distance=distance):
            @pl.when((z >= distance) & (z < n_kvh - 1))
            def _():
                z_copy(z - distance, block, z_up, z + 1).wait_send()

            @pl.when((z + distance < n_kvh) & (z > 0))
            def _():
                z_copy(z + distance, block, z_down, z - 1).wait_send()


def line_kernel(
    n_ctx, n_kvh, n_slash, n_vert,
    vert_ref, slash_ref, q_ref, k_ref, v_ref, w_ref, out_ref,
    kv_buf, w_buf, att_buf, kg, vg, bias, q_raw, q_wide, q_buf, acc, out_buf,
    mate_kv, mate_raw, mate_q, allow_out, allow_in, mate_bias,
    local_sem, kv_recv, kv_send, kv_fwd, w_recv, w_send, w_fwd, z_recv, z_up, z_down, out_sem,
    mate_recv, mate_send, mkv_recv, mkv_send, mkv_fwd,
):
    c = lax.axis_index("ctx")
    z = lax.axis_index("kvh")
    n_chip = n_ctx // CORES
    chip, core = c // CORES, c % CORES
    sibling = chip * CORES + (1 - core)
    blocks = k_ref.shape[0]
    tokens, heads, head_size = q_ref.shape
    kv_refs = (k_ref, v_ref)
    w_rows = w_ref.shape[0]
    n_slots = kg.shape[0] // BLK

    def peer(step):
        return lax.rem(chip + step, n_chip) * CORES + core

    def sibling_source(step):
        return lax.rem(chip + n_chip - step, n_chip) * CORES + (1 - core)

    def kv_at(part, owner):
        return kv_buf.at[part, pl.ds(owner * blocks, blocks)]

    half_rows = w_rows // 2

    def w_at(owner, half):
        first = pl.multiple_of(owner * w_rows + half * half_rows, half_rows)
        return w_buf.at[pl.ds(first, half_rows)]

    def own_rows(half):
        return w_ref.at[pl.ds(half * half_rows, half_rows)]

    def push(src, dst, send_sem, recv_sem, to_ctx, to_z):
        return pltpu.make_async_remote_copy(
            src_ref=src, dst_ref=dst, send_sem=send_sem, recv_sem=recv_sem,
            device_id=(to_ctx, to_z), device_id_type=pl.DeviceIdType.MESH,
        )

    own_q = pltpu.make_async_copy(q_ref, q_raw, local_sem.at[2])
    own_q.start()
    own_w = [
        pltpu.make_async_copy(own_rows(half), w_at(c, half), local_sem.at[3 + half])
        for half in (0, 1)
    ]

    barrier = pltpu.get_barrier_semaphore()

    def greet(to_ctx, to_z):
        pl.semaphore_signal(
            barrier, inc=1, device_id=(to_ctx, to_z), device_id_type=pl.DeviceIdType.MESH
        )

    @pl.loop(1, n_chip)
    def _(step):
        greet(peer(step), z)

    greet(sibling, z)

    @pl.when(z > 0)
    def _():
        greet(c, z - 1)

    @pl.when(z < n_kvh - 1)
    def _():
        greet(c, z + 1)

    last = n_kvh - 1
    at_end = (z == 0) | (z == last)
    in_middle = jnp.logical_not(at_end)
    mate = z + 1 - 2 * (z % 2)
    first_again = blocks - AGAIN

    inner = jnp.where(z > 0, 1, 0) + jnp.where(z < n_kvh - 1, 1, 0)
    lane = lax.broadcasted_iota(jnp.int32, (BLK, 2 * BLK), 1)
    row = lax.broadcasted_iota(jnp.int32, (BLK, 2 * BLK), 0)

    @pl.loop(0, blocks)
    def _(block):
        place = c * blocks + block
        fills = [jnp.float32(0.0)]
        for j in range(n_slash):
            fills.append(jnp.where(place - slash_ref[0, j] >= 0, 0.0, NEG_FILL))
        for j in range(n_vert):
            gap = place - vert_ref[0, j]
            fill = jnp.where(gap > 0, 0.0, NEG_FILL)
            for k in range(n_slash):
                fill = jnp.where(gap == slash_ref[0, k], NEG_FILL, fill)
            fills.append(fill)
        while len(fills) < n_slots:
            fills.append(jnp.float32(NEG_FILL))
        for j in range(0, n_slots, 2):
            fill = jnp.where(lane < BLK, fills[j], fills[j + 1])
            if j == 0:
                fill = jnp.where((lane < BLK) & (lane > row), NEG_FILL, fill)
            bias[block, :, j * BLK:(j + 2) * BLK] = fill

    key_block = lax.broadcasted_iota(jnp.int32, (8, 2 * BLK), 1)
    again_place = c * blocks + first_again + lax.broadcasted_iota(jnp.int32, (8, 2 * BLK), 0)
    kept = key_block == again_place
    for j in range(n_slash):
        kept = kept | (again_place - key_block == slash_ref[0, j])
    for j in range(n_vert):
        kept = kept | ((key_block == vert_ref[0, j]) & (key_block < again_place))
    allow_out[...] = jnp.where(kept, 1.0, 0.0)

    pl.semaphore_wait(barrier, n_chip + inner)

    square = n_chip == 4
    beside = (chip // 2) * 2 + (1 - chip % 2)
    behind = (1 - chip // 2) * 2 + chip % 2
    corner = n_chip - 1 - chip

    mate_pairs = (
        (k_ref, mate_kv.at[0, pl.ds(c * blocks, blocks)]),
        (v_ref, mate_kv.at[1, pl.ds(c * blocks, blocks)]),
        (allow_out, allow_in),
        (q_ref.at[pl.ds(first_again * BLK, AGAIN * BLK)], mate_raw),
    )

    def mate_copy(i):
        src, dst = mate_pairs[i]
        return push(src, dst, mate_send.at[i], mate_recv.at[i], c, mate)

    @pl.when(in_middle)
    def _():
        for i in range(len(mate_pairs)):
            mate_copy(i).start()

    own_kv = [
        pltpu.make_async_copy(kv_refs[part], kv_at(part, c), local_sem.at[part]) for part in (0, 1)
    ]

    def kv_direct(to_chip, part, slot):
        return push(
            kv_refs[part], kv_at(part, c), kv_send.at[part, slot], kv_recv.at[part, c],
            to_chip * CORES + core, z,
        )

    def kv_arrival(owner, part):
        rows = kv_at(part, owner)
        return push(rows, rows, kv_send.at[part, 0], kv_recv.at[part, owner], c, z)

    def kv_across(owner, part, slot):
        rows = kv_at(part, owner)
        return push(rows, rows, kv_fwd.at[part, slot], kv_recv.at[part, owner], sibling, z)

    def kv_corner(part):
        from_chip, to_chip = (beside, behind) if part == 0 else (behind, beside)
        owner = from_chip * CORES + core
        rows = kv_at(part, owner)
        return push(
            rows, rows, kv_send.at[part, 0], kv_recv.at[part, owner], to_chip * CORES + core, z
        )

    def kv_pass(chip_from, part, slot):
        owner = chip_from * CORES + core
        kv_arrival(owner, part).wait_recv()
        kv_across(owner, part, slot).start()

    own_across = [
        push(kv_refs[part], kv_at(part, c), kv_fwd.at[part, 0], kv_recv.at[part, c], sibling, z)
        for part in (0, 1)
    ]

    if square:
        for first in (0, 1):
            kv_direct(beside, first, 1).start()
            kv_direct(behind, 1 - first, 2).start()
    else:

        @pl.loop(1, n_chip)
        def _(step):
            for part in (0, 1):
                kv_direct(lax.rem(chip + step, n_chip), part, step).start()

    for part in (0, 1):
        own_across[part].start()
        own_kv[part].start()

    for part in (0, 1):
        own_kv[part].wait()

    if square:
        for part, chip_from, slot in ((0, beside, 1), (1, behind, 2)):
            kv_arrival(chip_from * CORES + core, part).wait_recv()
            kv_corner(part).start()
            kv_across(chip_from * CORES + core, part, slot).start()

    own_q.wait()

    @pl.loop(0, blocks)
    def _(block):
        first_row = pl.multiple_of(block * BLK, BLK)
        wide = q_raw[pl.ds(first_row, BLK)].astype(jnp.float32)
        q_wide[...] = wide.reshape(BLK * heads, head_size)
        for h in range(heads):
            q_buf[h, pl.ds(first_row, BLK), :] = q_wide[
                pl.ds(h, BLK, stride=heads), :
            ].astype(jnp.bfloat16)

    if square:
        kv_pass(beside, 1, 1)
        kv_pass(behind, 0, 2)
        for part in (0, 1):
            kv_pass(corner, part, 3)
    else:

        @pl.loop(1, n_chip)
        def _(step):
            for part in (0, 1):
                kv_pass(lax.rem(chip + step, n_chip), part, step)

    def mkv_at(part, chip_of, core_of):
        return mate_kv.at[part, pl.ds((chip_of * CORES + core_of) * blocks, blocks)]

    def mkv_copy(chip_of, part, sem, to_ctx):
        rows = mkv_at(part, chip_of, core)
        return push(rows, rows, sem, mkv_recv.at[part, chip_of * CORES + core], to_ctx, z)

    def mkv_direct(to_chip, part, slot):
        return mkv_copy(chip, part, mkv_send.at[part, slot], to_chip * CORES + core)

    def mkv_across(chip_of, part, slot):
        return mkv_copy(chip_of, part, mkv_fwd.at[part, slot], sibling)

    def mkv_corner(part):
        from_chip, to_chip = (beside, behind) if part == 0 else (behind, beside)
        return mkv_copy(from_chip, part, mkv_send.at[part, 0], to_chip * CORES + core)

    def mkv_arrival(chip_of, core_of, part):
        rows = mkv_at(part, chip_of, core_of)
        return push(
            rows, rows, mkv_send.at[part, 0], mkv_recv.at[part, chip_of * CORES + core_of],
            sibling, z,
        )

    @pl.when(at_end)
    def _():
        for i in (0, 1):
            mate_copy(i).wait_recv()
        for first in (0, 1):
            mkv_direct(beside, first, 1).start()
            mkv_direct(behind, 1 - first, 2).start()
        for part in (0, 1):
            mkv_across(chip, part, 0).start()

    def w_direct(to_chip, half, slot):
        return push(
            own_rows(half), w_at(c, half), w_send.at[slot, half], w_recv.at[c, half],
            to_chip * CORES + core, z,
        )

    def w_arrival(owner, half):
        return push(
            w_at(owner, half), w_at(owner, half), w_send.at[0, half], w_recv.at[owner, half], c, z
        )

    def w_across(owner, half, slot):
        return push(
            w_at(owner, half), w_at(owner, half), w_fwd.at[slot, half], w_recv.at[owner, half],
            sibling, z,
        )

    def w_corner(half):
        from_chip, to_chip = (beside, behind) if half == 0 else (behind, beside)
        owner = from_chip * CORES + core
        return push(
            w_at(owner, half), w_at(owner, half), w_send.at[0, half], w_recv.at[owner, half],
            to_chip * CORES + core, z,
        )

    w_direct(beside, 0, 1).start()
    w_direct(behind, 1, 2).start()

    own_w_across = [
        push(own_rows(half), w_at(c, half), w_fwd.at[0, half], w_recv.at[c, half], sibling, z)
        for half in (0, 1)
    ]
    for half in (0, 1):
        own_w_across[half].start()
        own_w[half].start()

    def w_pass(chip_from, half, slot):
        owner = chip_from * CORES + core
        w_arrival(owner, half).wait_recv()
        w_across(owner, half, slot).start()

    @pl.loop(0, n_chip)
    def _(step):
        for part in (0, 1):
            kv_arrival(sibling_source(step), part).wait_recv()

    def z_copy(owner, block, sems, to_z):
        rows = att_buf.at[owner, pl.ds(pl.multiple_of(block * BLK, BLK), BLK)]
        return push(rows, rows, sems.at[owner, block], z_recv.at[owner, block], c, to_z)

    def sent(block, owner, to_z):
        ends = ((owner == 1) & (to_z == 0)) | ((owner == last - 1) & (to_z == last))
        return jnp.logical_not(ends & (block >= first_again))

    def line_step(block, distance):
        @pl.when((z >= distance) & sent(block, z - distance, z))
        def _():
            z_copy(z - distance, block, z_up, z).wait_recv()

            if distance < n_kvh - 1:
                @pl.when(z < n_kvh - 1)
                def _():
                    z_copy(z - distance, block, z_up, z + 1).start()

        @pl.when((z + distance < n_kvh) & sent(block, z + distance, z))
        def _():
            z_copy(z + distance, block, z_down, z).wait_recv()

            if distance < n_kvh - 1:
                @pl.when(z > 0)
                def _():
                    z_copy(z + distance, block, z_down, z - 1).start()

    exponent_scale = math.log2(math.e) / math.sqrt(head_size)

    @pl.loop(0, blocks)
    def _(block):
        place = c * blocks + block
        picks = [place] + [jnp.maximum(place - slash_ref[0, j], 0) for j in range(n_slash)]
        picks += [vert_ref[0, j] for j in range(n_vert)]
        picks += [place] * (n_slots - len(picks))
        for j, pick in enumerate(picks):
            kg[j * BLK:(j + 1) * BLK, :] = kv_buf[0, pick]
            vg[j * BLK:(j + 1) * BLK, :] = kv_buf[1, pick]

        first_row = pl.multiple_of(block * BLK, BLK)
        part = heads // 2
        for half in range(2):
            rows = q_buf[half * part:(half + 1) * part, pl.ds(first_row, BLK), :]
            scores = lax.dot_general(
                rows.reshape(part * BLK, head_size), kg[...], (((1,), (1,)), ((), ())),
                preferred_element_type=jnp.float32,
            )
            scores = scores.reshape(part, BLK, n_slots * BLK) + bias[block][None]
            scores = scores.reshape(part * BLK, n_slots * BLK)
            peak = jnp.max(scores, axis=-1, keepdims=True)
            weights = jnp.exp2((scores - peak) * exponent_scale)
            total = jnp.sum(weights, axis=-1, keepdims=True)
            mixed = jnp.dot(
                weights.astype(jnp.bfloat16), vg[...], preferred_element_type=jnp.float32
            )
            mixed = (mixed / total).astype(jnp.bfloat16)
            for h in range(part):
                col = (half * part + h) * head_size
                att_buf[z, pl.ds(first_row, BLK), col:col + head_size] = mixed[
                    h * BLK:(h + 1) * BLK
                ]

        @pl.when((z < n_kvh - 1) & sent(block, z, z + 1))
        def _():
            z_copy(z, block, z_up, z + 1).start()

        @pl.when((z > 0) & sent(block, z, z - 1))
        def _():
            z_copy(z, block, z_down, z - 1).start()

        @pl.when(block == 1)
        def _():
            @pl.when(at_end)
            def _():
                for part, chip_from, slot in ((0, beside, 1), (1, behind, 2)):
                    mkv_arrival(chip_from, core, part).wait_recv()
                    mkv_corner(part).start()
                    mkv_across(chip_from, part, slot).start()

            w_direct(beside, 1, 1).start()
            w_direct(behind, 0, 2).start()

        @pl.when(in_middle & (block >= EARLY))
        def _():
            line_step(block - EARLY, 1)

    for half, chip_from, slot in ((0, beside, 1), (1, behind, 2)):
        w_arrival(chip_from * CORES + core, half).wait_recv()
        w_corner(half).start()
        w_across(chip_from * CORES + core, half, slot).start()

    acc[...] = jnp.zeros_like(acc)

    @pl.when(in_middle)
    def _():
        @pl.loop(blocks - EARLY, blocks)
        def _(block):
            line_step(block, 1)

    @pl.when(at_end)
    def _():
        mkv_pass = ((beside, 1, 1), (behind, 0, 2), (corner, 0, 3), (corner, 1, 3))
        for chip_from, part, slot in mkv_pass:
            mkv_arrival(chip_from, core, part).wait_recv()
            mkv_across(chip_from, part, slot).start()
        for i in (2, 3):
            mate_copy(i).wait_recv()

        @pl.loop(0, n_chip)
        def _(chip_of):
            for part in (0, 1):
                mkv_arrival(chip_of, 1 - core, part).wait_recv()

        @pl.loop(0, AGAIN)
        def _(b):
            first_row = pl.multiple_of(b * BLK, BLK)
            wide = mate_raw[pl.ds(first_row, BLK)].astype(jnp.float32)
            q_wide[...] = wide.reshape(BLK * heads, head_size)
            for h in range(heads):
                mate_q[h, pl.ds(first_row, BLK), :] = q_wide[
                    pl.ds(h, BLK, stride=heads), :
                ].astype(jnp.bfloat16)

        keys = n_ctx * blocks * BLK
        spread = (
            lax.broadcasted_iota(jnp.int32, (2 * BLK, keys), 1) // BLK
            == lax.broadcasted_iota(jnp.int32, (2 * BLK, keys), 0)
        )
        allowed = jnp.dot(
            allow_in[...].astype(jnp.bfloat16),
            jnp.where(spread, 1.0, 0.0).astype(jnp.bfloat16),
            preferred_element_type=jnp.float32,
        )
        key_at = lax.broadcasted_iota(jnp.int32, (BLK, keys), 1)
        query_row = lax.broadcasted_iota(jnp.int32, (BLK, keys), 0)
        for b in range(AGAIN):
            query_at = (c * blocks + first_again + b) * BLK + query_row
            mate_bias[b] = jnp.where(
                (allowed[b:b + 1] > 0.5) & (key_at <= query_at), 0.0, NEG_FILL
            )

        @pl.loop(0, AGAIN * 4)
        def _(i):
            b, quarter = i // 4, i % 4
            part = heads // 4
            from_row = pl.multiple_of(b * BLK, BLK)
            rows = mate_q[pl.ds(quarter * part, part), pl.ds(from_row, BLK), :]
            scores = lax.dot_general(
                rows.reshape(part * BLK, head_size), mate_kv[0].reshape(keys, head_size),
                (((1,), (1,)), ((), ())), preferred_element_type=jnp.float32,
            )
            scores = scores.reshape(part, BLK, keys) + mate_bias[b][None]
            scores = scores.reshape(part * BLK, keys)
            peak = jnp.max(scores, axis=-1, keepdims=True)
            weights = jnp.exp2((scores - peak) * exponent_scale)
            total = jnp.sum(weights, axis=-1, keepdims=True)
            mixed = jnp.dot(
                weights.astype(jnp.bfloat16), mate_kv[1].reshape(keys, head_size),
                preferred_element_type=jnp.float32,
            )
            mixed = (mixed / total).astype(jnp.bfloat16)
            to_row = pl.multiple_of((first_again + b) * BLK, BLK)
            for h in range(part):
                col = pl.multiple_of((quarter * part + h) * head_size, head_size)
                att_buf[mate, pl.ds(to_row, BLK), pl.ds(col, head_size)] = mixed[
                    h * BLK:(h + 1) * BLK
                ]

    depth = att_buf.shape[2]
    tile = 256
    n_tiles = out_ref.shape[1] // tile
    parts = OUT_PARTS
    part_rows = tokens // parts
    part_blocks = blocks // parts

    def out_copy(p):
        rows = pl.ds(pl.multiple_of(p * part_rows, part_rows), part_rows)
        return pltpu.make_async_copy(out_buf.at[rows], out_ref.at[rows], out_sem.at[p])

    def product(owner, rows, cols):
        return jnp.dot(
            att_buf[owner, rows, :],
            w_buf[pl.ds(pl.multiple_of(owner * depth, depth), depth), cols],
            preferred_element_type=jnp.float32,
        )

    def add_product(owner):
        @pl.loop(0, n_tiles)
        def _(j):
            cols = pl.ds(pl.multiple_of(j * tile, tile), tile)
            acc[:, cols] += product(owner, slice(None), cols)

    far = last - z

    def add_in_full(chip_of):
        @pl.when(jnp.logical_not(at_end & (chip_of == far)))
        def _():
            add_product(chip_of)

    def w_ready(chip_of):
        for half in (0, 1):
            w_arrival(chip_of * CORES + (1 - core), half).wait_recv()

    @pl.when(in_middle)
    def _():
        @pl.loop(0, AHEAD)
        def _(block):
            line_step(block, 2)

    w_pass(beside, 1, 1)
    w_pass(behind, 0, 2)

    @pl.when(in_middle)
    def _():
        @pl.loop(AHEAD, blocks)
        def _(block):
            line_step(block, 2)

    @pl.when(at_end)
    def _():
        for distance in (1, 2):

            @pl.loop(0, blocks)
            def _(block, distance=distance):
                line_step(block, distance)

    for half in (0, 1):
        own_w[half].wait()
    for chip_of in (chip, beside, behind):
        w_ready(chip_of)
        add_in_full(chip_of)

    for half in (0, 1):
        w_pass(corner, half, 3)
    w_ready(corner)
    add_in_full(corner)

    @pl.when(at_end)
    def _():
        @pl.loop(0, parts)
        def _(p):
            @pl.loop(0, part_blocks)
            def _(b):
                line_step(p * part_blocks + b, last)

            rows = pl.ds(pl.multiple_of(p * part_rows, part_rows), part_rows)

            @pl.loop(0, n_tiles)
            def _(j):
                cols = pl.ds(pl.multiple_of(j * tile, tile), tile)
                total = acc[rows, cols] + product(far, rows, cols)
                out_buf[rows, cols] = total.astype(out_ref.dtype)

            out_copy(p).start()

    @pl.when(jnp.logical_not(at_end))
    def _():
        out_buf[...] = acc[...].astype(out_ref.dtype)

        @pl.loop(0, parts)
        def _(p):
            out_copy(p).start()

    @pl.loop(0, parts)
    def _(p):
        out_copy(p).wait()

    for part in (0, 1):
        own_across[part].wait_send()
    for half in (0, 1):
        own_w_across[half].wait_send()

    @pl.loop(1, n_chip)
    def _(step):
        for part in (0, 1):
            kv_across(c, part, step).wait_send()
        for half in (0, 1):
            w_across(c, half, step).wait_send()

    if square:
        for half in (0, 1):
            w_corner(half).wait_send()
            w_direct(beside, half, 1).wait_send()
            w_direct(behind, half, 2).wait_send()
            kv_corner(half).wait_send()
            kv_direct(beside, half, 1).wait_send()
            kv_direct(behind, half, 2).wait_send()
    else:

        @pl.loop(1, n_chip)
        def _(step):
            for half in (0, 1):
                w_direct(lax.rem(chip + step, n_chip), half, step).wait_send()
                kv_direct(lax.rem(chip + step, n_chip), half, step).wait_send()

    for distance in range(n_kvh):

        @pl.loop(0, blocks)
        def _(block, distance=distance):
            @pl.when((z >= distance) & (z < n_kvh - 1) & sent(block, z - distance, z + 1))
            def _():
                z_copy(z - distance, block, z_up, z + 1).wait_send()

            @pl.when((z + distance < n_kvh) & (z > 0) & sent(block, z + distance, z - 1))
            def _():
                z_copy(z + distance, block, z_down, z - 1).wait_send()

    @pl.when(in_middle)
    def _():
        for i in range(len(mate_pairs)):
            mate_copy(i).wait_send()

    @pl.when(at_end)
    def _():
        for part in (0, 1):
            mkv_corner(part).wait_send()
            mkv_direct(beside, part, 1).wait_send()
            mkv_direct(behind, part, 2).wait_send()
            for slot in range(n_chip):
                mkv_across(chip, part, slot).wait_send()


def solution(mesh):
    n_ctx, n_kvh = mesh.shape["ctx"], mesh.shape["kvh"]

    def on_device(queries, keys, values, vert_blocks, slash_offsets, out_weight):
        tokens, heads, head_size = queries.shape
        blocks = tokens // BLK
        n_slash, n_vert = slash_offsets.shape[1], vert_blocks.shape[1]
        n_slots = 1 + n_slash + n_vert
        n_slots += n_slots % 2
        w_rows, _, w_cols = out_weight.shape
        n_chip = n_ctx // CORES
        k = keys.reshape(blocks, BLK, head_size)
        v = values.reshape(blocks, BLK, head_size)
        dma = pltpu.SemaphoreType.DMA
        shared = [
            pltpu.VMEM((n_slots * BLK, head_size), jnp.bfloat16),
            pltpu.VMEM((n_slots * BLK, head_size), jnp.bfloat16),
            pltpu.VMEM((blocks, BLK, n_slots * BLK), jnp.float32),
            pltpu.VMEM((tokens, heads, head_size), jnp.bfloat16),
            pltpu.VMEM((BLK * heads, head_size), jnp.float32),
            pltpu.VMEM((heads, tokens, head_size), jnp.bfloat16),
        ]
        kv_buf = pltpu.VMEM((2, n_ctx * blocks, BLK, head_size), jnp.bfloat16)
        scratch = [
            kv_buf,
            pltpu.VMEM((n_ctx * w_rows, w_cols), jnp.bfloat16),
            pltpu.VMEM((n_kvh, tokens, heads * head_size), jnp.bfloat16),
            *shared,
            pltpu.VMEM((tokens, w_cols), jnp.float32),
            pltpu.VMEM((tokens, w_cols), jnp.bfloat16),
        ]
        sems = [
            dma((5,)),
            dma((2, n_ctx)),
            dma((2, n_chip)),
            dma((2, n_chip)),
            dma((n_ctx, 2)),
            dma((n_chip, 2)),
            dma((n_chip, 2)),
            dma((n_kvh, blocks)),
            dma((n_kvh, blocks)),
            dma((n_kvh, blocks)),
        ]
        if n_chip == 4 and n_kvh == 4 and n_ctx * blocks <= 2 * BLK:
            body = functools.partial(line_kernel, n_ctx, n_kvh, n_slash, n_vert)
            scratch += [
                kv_buf,
                pltpu.VMEM((AGAIN * BLK, heads, head_size), jnp.bfloat16),
                pltpu.VMEM((heads, AGAIN * BLK, head_size), jnp.bfloat16),
                pltpu.VMEM((8, 2 * BLK), jnp.float32),
                pltpu.VMEM((8, 2 * BLK), jnp.float32),
                pltpu.VMEM((AGAIN, BLK, n_ctx * tokens), jnp.float32),
                *sems,
                dma((OUT_PARTS,)),
                dma((4,)),
                dma((4,)),
                dma((2, n_ctx)),
                dma((2, n_chip)),
                dma((2, n_chip)),
            ]
        else:
            body = functools.partial(kernel, n_ctx, n_kvh, n_slash, n_vert)
            scratch += [*sems, dma((2,))]
        return pl.pallas_call(
            body,
            out_shape=jax.ShapeDtypeStruct((tokens, w_cols), jnp.bfloat16),
            in_specs=[
                pl.BlockSpec(memory_space=pltpu.SMEM),
                pl.BlockSpec(memory_space=pltpu.SMEM),
                pl.BlockSpec(memory_space=pl.ANY),
                pl.BlockSpec(memory_space=pl.ANY),
                pl.BlockSpec(memory_space=pl.ANY),
                pl.BlockSpec(memory_space=pl.ANY),
            ],
            out_specs=pl.BlockSpec(memory_space=pl.ANY),
            scratch_shapes=scratch,
            compiler_params=pltpu.CompilerParams(
                collective_id=0, has_side_effects=True, vmem_limit_bytes=56 * 2**20
            ),
        )(vert_blocks, slash_offsets, queries, k, v, out_weight.reshape(w_rows, w_cols))

    return jax.shard_map(
        on_device,
        mesh=mesh,
        in_specs=(
            P("ctx", "kvh", None),
            P("ctx", "kvh", None),
            P("ctx", "kvh", None),
            P("kvh", None),
            P("kvh", None),
            P("ctx", "kvh", None),
        ),
        out_specs=P("ctx", "kvh"),
        check_vma=False,
    )
```

```python
import functools
import math

import jax
import jax.numpy as jnp
from jax import lax
from jax.experimental import pallas as pl
from jax.experimental.pallas import tpu as pltpu
from jax.sharding import PartitionSpec as P

BLK = 64
CORES = 2
NEG_FILL = -1e30
AGAIN = 3
EARLY = 3
OUT_PARTS = 3


def kernel(
    n_ctx, n_kvh, n_slash, n_vert,
    vert_ref, slash_ref, q_ref, k_ref, v_ref, w_ref, out_ref,
    kv_buf, w_buf, att_buf, kg, vg, bias, q_raw, q_wide, q_buf, acc, out_buf,
    local_sem, kv_recv, kv_send, kv_fwd, w_recv, w_send, w_fwd, z_recv, z_up, z_down, out_sem,
):
    c = lax.axis_index("ctx")
    z = lax.axis_index("kvh")
    n_chip = n_ctx // CORES
    chip, core = c // CORES, c % CORES
    sibling = chip * CORES + (1 - core)
    blocks = k_ref.shape[0]
    tokens, heads, head_size = q_ref.shape
    kv_refs = (k_ref, v_ref)
    w_rows = w_ref.shape[0]
    n_slots = kg.shape[0] // BLK

    def peer(step):
        return lax.rem(chip + step, n_chip) * CORES + core

    def sibling_source(step):
        return lax.rem(chip + n_chip - step, n_chip) * CORES + (1 - core)

    def kv_at(part, owner):
        return kv_buf.at[part, pl.ds(owner * blocks, blocks)]

    half_rows = w_rows // 2

    def w_at(owner, half):
        first = pl.multiple_of(owner * w_rows + half * half_rows, half_rows)
        return w_buf.at[pl.ds(first, half_rows)]

    def own_rows(half):
        return w_ref.at[pl.ds(half * half_rows, half_rows)]

    def push(src, dst, send_sem, recv_sem, to_ctx, to_z):
        return pltpu.make_async_remote_copy(
            src_ref=src, dst_ref=dst, send_sem=send_sem, recv_sem=recv_sem,
            device_id=(to_ctx, to_z), device_id_type=pl.DeviceIdType.MESH,
        )

    own_q = pltpu.make_async_copy(q_ref, q_raw, local_sem.at[2])
    own_q.start()
    own_w = [
        pltpu.make_async_copy(own_rows(half), w_at(c, half), local_sem.at[3 + half])
        for half in (0, 1)
    ]

    barrier = pltpu.get_barrier_semaphore()

    def greet(to_ctx, to_z):
        pl.semaphore_signal(
            barrier, inc=1, device_id=(to_ctx, to_z), device_id_type=pl.DeviceIdType.MESH
        )

    @pl.loop(1, n_chip)
    def _(step):
        greet(peer(step), z)

    greet(sibling, z)

    @pl.when(z > 0)
    def _():
        greet(c, z - 1)

    @pl.when(z < n_kvh - 1)
    def _():
        greet(c, z + 1)

    inner = jnp.where(z > 0, 1, 0) + jnp.where(z < n_kvh - 1, 1, 0)
    lane = lax.broadcasted_iota(jnp.int32, (BLK, 2 * BLK), 1)
    row = lax.broadcasted_iota(jnp.int32, (BLK, 2 * BLK), 0)

    @pl.loop(0, blocks)
    def _(block):
        place = c * blocks + block
        fills = [jnp.float32(0.0)]
        for j in range(n_slash):
            fills.append(jnp.where(place - slash_ref[0, j] >= 0, 0.0, NEG_FILL))
        for j in range(n_vert):
            gap = place - vert_ref[0, j]
            fill = jnp.where(gap > 0, 0.0, NEG_FILL)
            for k in range(n_slash):
                fill = jnp.where(gap == slash_ref[0, k], NEG_FILL, fill)
            fills.append(fill)
        while len(fills) < n_slots:
            fills.append(jnp.float32(NEG_FILL))
        for j in range(0, n_slots, 2):
            fill = jnp.where(lane < BLK, fills[j], fills[j + 1])
            if j == 0:
                fill = jnp.where((lane < BLK) & (lane > row), NEG_FILL, fill)
            bias[block, :, j * BLK:(j + 2) * BLK] = fill

    pl.semaphore_wait(barrier, n_chip + inner)

    square = n_chip == 4
    beside = (chip // 2) * 2 + (1 - chip % 2)
    behind = (1 - chip // 2) * 2 + chip % 2
    corner = n_chip - 1 - chip

    own_kv = [
        pltpu.make_async_copy(kv_refs[part], kv_at(part, c), local_sem.at[part]) for part in (0, 1)
    ]

    def kv_direct(to_chip, part, slot):
        return push(
            kv_refs[part], kv_at(part, c), kv_send.at[part, slot], kv_recv.at[part, c],
            to_chip * CORES + core, z,
        )

    def kv_arrival(owner, part):
        rows = kv_at(part, owner)
        return push(rows, rows, kv_send.at[part, 0], kv_recv.at[part, owner], c, z)

    def kv_across(owner, part, slot):
        rows = kv_at(part, owner)
        return push(rows, rows, kv_fwd.at[part, slot], kv_recv.at[part, owner], sibling, z)

    def kv_corner(part):
        from_chip, to_chip = (beside, behind) if part == 0 else (behind, beside)
        owner = from_chip * CORES + core
        rows = kv_at(part, owner)
        return push(
            rows, rows, kv_send.at[part, 0], kv_recv.at[part, owner], to_chip * CORES + core, z
        )

    def kv_pass(chip_from, part, slot):
        owner = chip_from * CORES + core
        kv_arrival(owner, part).wait_recv()
        kv_across(owner, part, slot).start()

    own_across = [
        push(kv_refs[part], kv_at(part, c), kv_fwd.at[part, 0], kv_recv.at[part, c], sibling, z)
        for part in (0, 1)
    ]

    if square:
        for first in (0, 1):
            kv_direct(beside, first, 1).start()
            kv_direct(behind, 1 - first, 2).start()
    else:

        @pl.loop(1, n_chip)
        def _(step):
            for part in (0, 1):
                kv_direct(lax.rem(chip + step, n_chip), part, step).start()

    for part in (0, 1):
        own_across[part].start()
        own_kv[part].start()

    for part in (0, 1):
        own_kv[part].wait()

    if square:
        for part, chip_from, slot in ((0, beside, 1), (1, behind, 2)):
            kv_arrival(chip_from * CORES + core, part).wait_recv()
            kv_corner(part).start()
            kv_across(chip_from * CORES + core, part, slot).start()

    own_q.wait()

    @pl.loop(0, blocks)
    def _(block):
        first_row = pl.multiple_of(block * BLK, BLK)
        wide = q_raw[pl.ds(first_row, BLK)].astype(jnp.float32)
        q_wide[...] = wide.reshape(BLK * heads, head_size)
        for h in range(heads):
            q_buf[h, pl.ds(first_row, BLK), :] = q_wide[
                pl.ds(h, BLK, stride=heads), :
            ].astype(jnp.bfloat16)

    if square:
        kv_pass(beside, 1, 1)
        kv_pass(behind, 0, 2)
        for part in (0, 1):
            kv_pass(corner, part, 3)
    else:

        @pl.loop(1, n_chip)
        def _(step):
            for part in (0, 1):
                kv_pass(lax.rem(chip + step, n_chip), part, step)

    def w_direct(to_chip, half, slot):
        return push(
            own_rows(half), w_at(c, half), w_send.at[slot, half], w_recv.at[c, half],
            to_chip * CORES + core, z,
        )

    def w_arrival(owner, half):
        return push(
            w_at(owner, half), w_at(owner, half), w_send.at[0, half], w_recv.at[owner, half], c, z
        )

    def w_across(owner, half, slot):
        return push(
            w_at(owner, half), w_at(owner, half), w_fwd.at[slot, half], w_recv.at[owner, half],
            sibling, z,
        )

    def w_corner(half):
        from_chip, to_chip = (beside, behind) if half == 0 else (behind, beside)
        owner = from_chip * CORES + core
        return push(
            w_at(owner, half), w_at(owner, half), w_send.at[0, half], w_recv.at[owner, half],
            to_chip * CORES + core, z,
        )

    if square:
        for first in (0, 1):
            w_direct(beside, first, 1).start()
            w_direct(behind, 1 - first, 2).start()
    else:

        @pl.loop(1, n_chip)
        def _(step):
            for half in (0, 1):
                w_direct(lax.rem(chip + step, n_chip), half, step).start()

    own_w_across = [
        push(own_rows(half), w_at(c, half), w_fwd.at[0, half], w_recv.at[c, half], sibling, z)
        for half in (0, 1)
    ]
    for half in (0, 1):
        own_w_across[half].start()
        own_w[half].start()

    def w_pass(chip_from, half, slot):
        owner = chip_from * CORES + core
        w_arrival(owner, half).wait_recv()
        w_across(owner, half, slot).start()

    @pl.loop(0, n_chip)
    def _(step):
        for part in (0, 1):
            kv_arrival(sibling_source(step), part).wait_recv()

    def z_copy(owner, block, sems, to_z):
        rows = att_buf.at[owner, pl.ds(pl.multiple_of(block * BLK, BLK), BLK)]
        return push(rows, rows, sems.at[owner, block], z_recv.at[owner, block], c, to_z)

    exponent_scale = math.log2(math.e) / math.sqrt(head_size)

    @pl.loop(0, blocks)
    def _(block):
        place = c * blocks + block
        picks = [place] + [jnp.maximum(place - slash_ref[0, j], 0) for j in range(n_slash)]
        picks += [vert_ref[0, j] for j in range(n_vert)]
        picks += [place] * (n_slots - len(picks))
        for j, pick in enumerate(picks):
            kg[j * BLK:(j + 1) * BLK, :] = kv_buf[0, pick]
            vg[j * BLK:(j + 1) * BLK, :] = kv_buf[1, pick]

        first_row = pl.multiple_of(block * BLK, BLK)
        part = heads // 2
        for half in range(2):
            rows = q_buf[half * part:(half + 1) * part, pl.ds(first_row, BLK), :]
            scores = lax.dot_general(
                rows.reshape(part * BLK, head_size), kg[...], (((1,), (1,)), ((), ())),
                preferred_element_type=jnp.float32,
            )
            scores = scores.reshape(part, BLK, n_slots * BLK) + bias[block][None]
            scores = scores.reshape(part * BLK, n_slots * BLK)
            peak = jnp.max(scores, axis=-1, keepdims=True)
            weights = jnp.exp2((scores - peak) * exponent_scale)
            total = jnp.sum(weights, axis=-1, keepdims=True)
            mixed = jnp.dot(
                weights.astype(jnp.bfloat16), vg[...], preferred_element_type=jnp.float32
            )
            mixed = (mixed / total).astype(jnp.bfloat16)
            for h in range(part):
                col = (half * part + h) * head_size
                att_buf[z, pl.ds(first_row, BLK), col:col + head_size] = mixed[
                    h * BLK:(h + 1) * BLK
                ]

        @pl.when(z < n_kvh - 1)
        def _():
            z_copy(z, block, z_up, z + 1).start()

        @pl.when(z > 0)
        def _():
            z_copy(z, block, z_down, z - 1).start()

    def line_step(block, distance):
        @pl.when(z >= distance)
        def _():
            z_copy(z - distance, block, z_up, z).wait_recv()

            if distance < n_kvh - 1:
                @pl.when(z < n_kvh - 1)
                def _():
                    z_copy(z - distance, block, z_up, z + 1).start()

        @pl.when(z + distance < n_kvh)
        def _():
            z_copy(z + distance, block, z_down, z).wait_recv()

            if distance < n_kvh - 1:
                @pl.when(z > 0)
                def _():
                    z_copy(z + distance, block, z_down, z - 1).start()

    if square:
        for half, chip_from, slot in ((0, beside, 1), (1, behind, 2)):
            w_arrival(chip_from * CORES + core, half).wait_recv()
            w_corner(half).start()
            w_across(chip_from * CORES + core, half, slot).start()

    for distance in range(1, n_kvh - 1):

        @pl.loop(0, blocks)
        def _(block, distance=distance):
            line_step(block, distance)

        if square and distance == 1:
            w_pass(beside, 1, 1)
            w_pass(behind, 0, 2)

    if square:
        for half in (0, 1):
            w_pass(corner, half, 3)
    else:

        @pl.loop(1, n_chip)
        def _(step):
            for half in (0, 1):
                w_pass(lax.rem(chip + step, n_chip), half, step)

    @pl.loop(0, n_chip)
    def _(step):
        for half in (0, 1):
            w_arrival(sibling_source(step), half).wait_recv()

    for half in (0, 1):
        own_w[half].wait()

    depth = att_buf.shape[2]
    tile = 256
    n_tiles = out_ref.shape[1] // tile
    parts = 2
    part_rows = tokens // parts
    part_blocks = blocks // parts

    def out_copy(p):
        rows = pl.ds(pl.multiple_of(p * part_rows, part_rows), part_rows)
        return pltpu.make_async_copy(out_buf.at[rows], out_ref.at[rows], out_sem.at[p])

    def product(owner, rows, cols):
        return jnp.dot(
            att_buf[owner, rows, :],
            w_buf[pl.ds(pl.multiple_of(owner * depth, depth), depth), cols],
            preferred_element_type=jnp.float32,
        )

    def add_product(owner):
        @pl.loop(0, n_tiles)
        def _(j):
            cols = pl.ds(pl.multiple_of(j * tile, tile), tile)
            acc[:, cols] += product(owner, slice(None), cols)

    @pl.loop(0, n_tiles)
    def _(j):
        cols = pl.ds(pl.multiple_of(j * tile, tile), tile)
        acc[:, cols] = product(z, slice(None), cols)

    for distance in range(1, n_kvh - 1):

        @pl.when(z >= distance)
        def _(distance=distance):
            add_product(z - distance)

        @pl.when(z + distance < n_kvh)
        def _(distance=distance):
            add_product(z + distance)

    last = n_kvh - 1
    at_end = (z == 0) | (z == last)
    far = last - z

    @pl.when(at_end)
    def _():
        @pl.loop(0, parts)
        def _(p):
            @pl.loop(0, part_blocks)
            def _(b):
                line_step(p * part_blocks + b, last)

            rows = pl.ds(pl.multiple_of(p * part_rows, part_rows), part_rows)

            @pl.loop(0, n_tiles)
            def _(j):
                cols = pl.ds(pl.multiple_of(j * tile, tile), tile)
                total = acc[rows, cols] + product(far, rows, cols)
                out_buf[rows, cols] = total.astype(out_ref.dtype)

            out_copy(p).start()

    @pl.when(jnp.logical_not(at_end))
    def _():
        out_buf[...] = acc[...].astype(out_ref.dtype)

        @pl.loop(0, parts)
        def _(p):
            out_copy(p).start()

    @pl.loop(0, parts)
    def _(p):
        out_copy(p).wait()

    for part in (0, 1):
        own_across[part].wait_send()
    for half in (0, 1):
        own_w_across[half].wait_send()

    @pl.loop(1, n_chip)
    def _(step):
        for part in (0, 1):
            kv_across(c, part, step).wait_send()
        for half in (0, 1):
            w_across(c, half, step).wait_send()

    if square:
        for half in (0, 1):
            w_corner(half).wait_send()
            w_direct(beside, half, 1).wait_send()
            w_direct(behind, half, 2).wait_send()
            kv_corner(half).wait_send()
            kv_direct(beside, half, 1).wait_send()
            kv_direct(behind, half, 2).wait_send()
    else:

        @pl.loop(1, n_chip)
        def _(step):
            for half in (0, 1):
                w_direct(lax.rem(chip + step, n_chip), half, step).wait_send()
                kv_direct(lax.rem(chip + step, n_chip), half, step).wait_send()

    for distance in range(n_kvh):

        @pl.loop(0, blocks)
        def _(block, distance=distance):
            @pl.when((z >= distance) & (z < n_kvh - 1))
            def _():
                z_copy(z - distance, block, z_up, z + 1).wait_send()

            @pl.when((z + distance < n_kvh) & (z > 0))
            def _():
                z_copy(z + distance, block, z_down, z - 1).wait_send()


def line_kernel(
    n_ctx, n_kvh, n_slash, n_vert,
    vert_ref, slash_ref, q_ref, k_ref, v_ref, w_ref, out_ref,
    kv_buf, w_buf, att_buf, kg, vg, bias, q_raw, q_wide, q_buf, acc,
    mate_kv, mate_raw, mate_q, allow_out, allow_in, mate_bias,
    local_sem, kv_recv, kv_send, kv_fwd, w_recv, w_send, w_fwd, z_recv, z_up, z_down,
    mate_recv, mate_send, mkv_recv, mkv_send, mkv_fwd,
):
    c = lax.axis_index("ctx")
    z = lax.axis_index("kvh")
    n_chip = n_ctx // CORES
    chip, core = c // CORES, c % CORES
    sibling = chip * CORES + (1 - core)
    blocks = k_ref.shape[0]
    tokens, heads, head_size = q_ref.shape
    kv_refs = (k_ref, v_ref)
    w_rows = w_ref.shape[0]
    n_slots = kg.shape[0] // BLK

    def peer(step):
        return lax.rem(chip + step, n_chip) * CORES + core

    def sibling_source(step):
        return lax.rem(chip + n_chip - step, n_chip) * CORES + (1 - core)

    def kv_at(part, owner):
        return kv_buf.at[part, pl.ds(owner * blocks, blocks)]

    half_rows = w_rows // 2

    def w_at(owner, half):
        first = pl.multiple_of(owner * w_rows + half * half_rows, half_rows)
        return w_buf.at[pl.ds(first, half_rows)]

    def own_rows(half):
        return w_ref.at[pl.ds(half * half_rows, half_rows)]

    def push(src, dst, send_sem, recv_sem, to_ctx, to_z):
        return pltpu.make_async_remote_copy(
            src_ref=src, dst_ref=dst, send_sem=send_sem, recv_sem=recv_sem,
            device_id=(to_ctx, to_z), device_id_type=pl.DeviceIdType.MESH,
        )

    own_q = pltpu.make_async_copy(q_ref, q_raw, local_sem.at[2])
    own_q.start()
    own_w = [
        pltpu.make_async_copy(own_rows(half), w_at(c, half), local_sem.at[3 + half])
        for half in (0, 1)
    ]

    barrier = pltpu.get_barrier_semaphore()

    def greet(to_ctx, to_z):
        pl.semaphore_signal(
            barrier, inc=1, device_id=(to_ctx, to_z), device_id_type=pl.DeviceIdType.MESH
        )

    @pl.loop(1, n_chip)
    def _(step):
        greet(peer(step), z)

    greet(sibling, z)

    @pl.when(z > 0)
    def _():
        greet(c, z - 1)

    @pl.when(z < n_kvh - 1)
    def _():
        greet(c, z + 1)

    last = n_kvh - 1
    at_end = (z == 0) | (z == last)
    in_middle = jnp.logical_not(at_end)
    mate = z + 1 - 2 * (z % 2)
    first_again = blocks - AGAIN

    inner = jnp.where(z > 0, 1, 0) + jnp.where(z < n_kvh - 1, 1, 0)
    lane = lax.broadcasted_iota(jnp.int32, (BLK, 2 * BLK), 1)
    row = lax.broadcasted_iota(jnp.int32, (BLK, 2 * BLK), 0)

    @pl.loop(0, blocks)
    def _(block):
        place = c * blocks + block
        fills = [jnp.float32(0.0)]
        for j in range(n_slash):
            fills.append(jnp.where(place - slash_ref[0, j] >= 0, 0.0, NEG_FILL))
        for j in range(n_vert):
            gap = place - vert_ref[0, j]
            fill = jnp.where(gap > 0, 0.0, NEG_FILL)
            for k in range(n_slash):
                fill = jnp.where(gap == slash_ref[0, k], NEG_FILL, fill)
            fills.append(fill)
        while len(fills) < n_slots:
            fills.append(jnp.float32(NEG_FILL))
        for j in range(0, n_slots, 2):
            fill = jnp.where(lane < BLK, fills[j], fills[j + 1])
            if j == 0:
                fill = jnp.where((lane < BLK) & (lane > row), NEG_FILL, fill)
            bias[block, :, j * BLK:(j + 2) * BLK] = fill

    key_block = lax.broadcasted_iota(jnp.int32, (8, 2 * BLK), 1)
    again_place = c * blocks + first_again + lax.broadcasted_iota(jnp.int32, (8, 2 * BLK), 0)
    kept = key_block == again_place
    for j in range(n_slash):
        kept = kept | (again_place - key_block == slash_ref[0, j])
    for j in range(n_vert):
        kept = kept | ((key_block == vert_ref[0, j]) & (key_block < again_place))
    allow_out[...] = jnp.where(kept, 1.0, 0.0)

    pl.semaphore_wait(barrier, n_chip + inner)

    square = n_chip == 4
    beside = (chip // 2) * 2 + (1 - chip % 2)
    behind = (1 - chip // 2) * 2 + chip % 2
    corner = n_chip - 1 - chip

    mate_pairs = (
        (k_ref, mate_kv.at[0, pl.ds(c * blocks, blocks)]),
        (v_ref, mate_kv.at[1, pl.ds(c * blocks, blocks)]),
        (allow_out, allow_in),
        (q_ref.at[pl.ds(first_again * BLK, AGAIN * BLK)], mate_raw),
    )

    def mate_copy(i):
        src, dst = mate_pairs[i]
        return push(src, dst, mate_send.at[i], mate_recv.at[i], c, mate)

    @pl.when(in_middle)
    def _():
        for i in range(len(mate_pairs)):
            mate_copy(i).start()

    own_kv = [
        pltpu.make_async_copy(kv_refs[part], kv_at(part, c), local_sem.at[part]) for part in (0, 1)
    ]

    def kv_direct(to_chip, part, slot):
        return push(
            kv_refs[part], kv_at(part, c), kv_send.at[part, slot], kv_recv.at[part, c],
            to_chip * CORES + core, z,
        )

    def kv_arrival(owner, part):
        rows = kv_at(part, owner)
        return push(rows, rows, kv_send.at[part, 0], kv_recv.at[part, owner], c, z)

    def kv_across(owner, part, slot):
        rows = kv_at(part, owner)
        return push(rows, rows, kv_fwd.at[part, slot], kv_recv.at[part, owner], sibling, z)

    def kv_corner(part):
        from_chip, to_chip = (beside, behind) if part == 0 else (behind, beside)
        owner = from_chip * CORES + core
        rows = kv_at(part, owner)
        return push(
            rows, rows, kv_send.at[part, 0], kv_recv.at[part, owner], to_chip * CORES + core, z
        )

    def kv_pass(chip_from, part, slot):
        owner = chip_from * CORES + core
        kv_arrival(owner, part).wait_recv()
        kv_across(owner, part, slot).start()

    own_across = [
        push(kv_refs[part], kv_at(part, c), kv_fwd.at[part, 0], kv_recv.at[part, c], sibling, z)
        for part in (0, 1)
    ]

    if square:
        for first in (0, 1):
            kv_direct(beside, first, 1).start()
            kv_direct(behind, 1 - first, 2).start()
    else:

        @pl.loop(1, n_chip)
        def _(step):
            for part in (0, 1):
                kv_direct(lax.rem(chip + step, n_chip), part, step).start()

    for part in (0, 1):
        own_across[part].start()
        own_kv[part].start()

    for part in (0, 1):
        own_kv[part].wait()

    if square:
        for part, chip_from, slot in ((0, beside, 1), (1, behind, 2)):
            kv_arrival(chip_from * CORES + core, part).wait_recv()
            kv_corner(part).start()
            kv_across(chip_from * CORES + core, part, slot).start()

    own_q.wait()

    @pl.loop(0, blocks)
    def _(block):
        first_row = pl.multiple_of(block * BLK, BLK)
        wide = q_raw[pl.ds(first_row, BLK)].astype(jnp.float32)
        q_wide[...] = wide.reshape(BLK * heads, head_size)
        for h in range(heads):
            q_buf[h, pl.ds(first_row, BLK), :] = q_wide[
                pl.ds(h, BLK, stride=heads), :
            ].astype(jnp.bfloat16)

    if square:
        kv_pass(beside, 1, 1)
        kv_pass(behind, 0, 2)
        for part in (0, 1):
            kv_pass(corner, part, 3)
    else:

        @pl.loop(1, n_chip)
        def _(step):
            for part in (0, 1):
                kv_pass(lax.rem(chip + step, n_chip), part, step)

    def mkv_at(part, chip_of, core_of):
        return mate_kv.at[part, pl.ds((chip_of * CORES + core_of) * blocks, blocks)]

    def mkv_copy(chip_of, part, sem, to_ctx):
        rows = mkv_at(part, chip_of, core)
        return push(rows, rows, sem, mkv_recv.at[part, chip_of * CORES + core], to_ctx, z)

    def mkv_direct(to_chip, part, slot):
        return mkv_copy(chip, part, mkv_send.at[part, slot], to_chip * CORES + core)

    def mkv_across(chip_of, part, slot):
        return mkv_copy(chip_of, part, mkv_fwd.at[part, slot], sibling)

    def mkv_corner(part):
        from_chip, to_chip = (beside, behind) if part == 0 else (behind, beside)
        return mkv_copy(from_chip, part, mkv_send.at[part, 0], to_chip * CORES + core)

    def mkv_arrival(chip_of, core_of, part):
        rows = mkv_at(part, chip_of, core_of)
        return push(
            rows, rows, mkv_send.at[part, 0], mkv_recv.at[part, chip_of * CORES + core_of],
            sibling, z,
        )

    @pl.when(at_end)
    def _():
        for i in (0, 1):
            mate_copy(i).wait_recv()
        for first in (0, 1):
            mkv_direct(beside, first, 1).start()
            mkv_direct(behind, 1 - first, 2).start()
        for part in (0, 1):
            mkv_across(chip, part, 0).start()

    def w_direct(to_chip, half, slot):
        return push(
            own_rows(half), w_at(c, half), w_send.at[slot, half], w_recv.at[c, half],
            to_chip * CORES + core, z,
        )

    def w_arrival(owner, half):
        return push(
            w_at(owner, half), w_at(owner, half), w_send.at[0, half], w_recv.at[owner, half], c, z
        )

    def w_across(owner, half, slot):
        return push(
            w_at(owner, half), w_at(owner, half), w_fwd.at[slot, half], w_recv.at[owner, half],
            sibling, z,
        )

    def w_corner(half):
        from_chip, to_chip = (beside, behind) if half == 0 else (behind, beside)
        owner = from_chip * CORES + core
        return push(
            w_at(owner, half), w_at(owner, half), w_send.at[0, half], w_recv.at[owner, half],
            to_chip * CORES + core, z,
        )

    w_direct(beside, 0, 1).start()
    w_direct(behind, 1, 2).start()

    own_w_across = [
        push(own_rows(half), w_at(c, half), w_fwd.at[0, half], w_recv.at[c, half], sibling, z)
        for half in (0, 1)
    ]
    for half in (0, 1):
        own_w_across[half].start()
        own_w[half].start()

    def w_pass(chip_from, half, slot):
        owner = chip_from * CORES + core
        w_arrival(owner, half).wait_recv()
        w_across(owner, half, slot).start()

    @pl.loop(0, n_chip)
    def _(step):
        for part in (0, 1):
            kv_arrival(sibling_source(step), part).wait_recv()

    def z_copy(owner, block, sems, to_z):
        rows = att_buf.at[owner, pl.ds(pl.multiple_of(block * BLK, BLK), BLK)]
        return push(rows, rows, sems.at[owner, block], z_recv.at[owner, block], c, to_z)

    def sent(block, owner, to_z):
        ends = ((owner == 1) & (to_z == 0)) | ((owner == last - 1) & (to_z == last))
        return jnp.logical_not(ends & (block >= first_again))

    def line_step(block, distance):
        @pl.when((z >= distance) & sent(block, z - distance, z))
        def _():
            z_copy(z - distance, block, z_up, z).wait_recv()

            if distance < n_kvh - 1:
                @pl.when(z < n_kvh - 1)
                def _():
                    z_copy(z - distance, block, z_up, z + 1).start()

        @pl.when((z + distance < n_kvh) & sent(block, z + distance, z))
        def _():
            z_copy(z + distance, block, z_down, z).wait_recv()

            if distance < n_kvh - 1:
                @pl.when(z > 0)
                def _():
                    z_copy(z + distance, block, z_down, z - 1).start()

    exponent_scale = math.log2(math.e) / math.sqrt(head_size)

    @pl.loop(0, blocks)
    def _(block):
        place = c * blocks + block
        picks = [place] + [jnp.maximum(place - slash_ref[0, j], 0) for j in range(n_slash)]
        picks += [vert_ref[0, j] for j in range(n_vert)]
        picks += [place] * (n_slots - len(picks))
        for j, pick in enumerate(picks):
            kg[j * BLK:(j + 1) * BLK, :] = kv_buf[0, pick]
            vg[j * BLK:(j + 1) * BLK, :] = kv_buf[1, pick]

        first_row = pl.multiple_of(block * BLK, BLK)
        part = heads // 2
        for half in range(2):
            rows = q_buf[half * part:(half + 1) * part, pl.ds(first_row, BLK), :]
            scores = lax.dot_general(
                rows.reshape(part * BLK, head_size), kg[...], (((1,), (1,)), ((), ())),
                preferred_element_type=jnp.float32,
            )
            scores = scores.reshape(part, BLK, n_slots * BLK) + bias[block][None]
            scores = scores.reshape(part * BLK, n_slots * BLK)
            peak = jnp.max(scores, axis=-1, keepdims=True)
            weights = jnp.exp2((scores - peak) * exponent_scale)
            total = jnp.sum(weights, axis=-1, keepdims=True)
            mixed = jnp.dot(
                weights.astype(jnp.bfloat16), vg[...], preferred_element_type=jnp.float32
            )
            mixed = (mixed / total).astype(jnp.bfloat16)
            for h in range(part):
                col = (half * part + h) * head_size
                att_buf[z, pl.ds(first_row, BLK), col:col + head_size] = mixed[
                    h * BLK:(h + 1) * BLK
                ]

        @pl.when((z < n_kvh - 1) & sent(block, z, z + 1))
        def _():
            z_copy(z, block, z_up, z + 1).start()

        @pl.when((z > 0) & sent(block, z, z - 1))
        def _():
            z_copy(z, block, z_down, z - 1).start()

        @pl.when(block == 1)
        def _():
            @pl.when(at_end)
            def _():
                for part, chip_from, slot in ((0, beside, 1), (1, behind, 2)):
                    mkv_arrival(chip_from, core, part).wait_recv()
                    mkv_corner(part).start()
                    mkv_across(chip_from, part, slot).start()

            w_direct(beside, 1, 1).start()
            w_direct(behind, 0, 2).start()

        @pl.when(in_middle & (block >= EARLY))
        def _():
            line_step(block - EARLY, 1)

    for half, chip_from, slot in ((0, beside, 1), (1, behind, 2)):
        w_arrival(chip_from * CORES + core, half).wait_recv()
        w_corner(half).start()
        w_across(chip_from * CORES + core, half, slot).start()

    acc[...] = jnp.zeros_like(acc)

    @pl.when(in_middle)
    def _():
        @pl.loop(0, EARLY)
        def _(block):
            line_step(blocks - EARLY + block, 1)
            line_step(block, 2)

    @pl.when(at_end)
    def _():
        mkv_pass = ((beside, 1, 1), (behind, 0, 2), (corner, 0, 3), (corner, 1, 3))
        for chip_from, part, slot in mkv_pass:
            mkv_arrival(chip_from, core, part).wait_recv()
            mkv_across(chip_from, part, slot).start()
        for i in (2, 3):
            mate_copy(i).wait_recv()

        @pl.loop(0, n_chip)
        def _(chip_of):
            for part in (0, 1):
                mkv_arrival(chip_of, 1 - core, part).wait_recv()

        @pl.loop(0, AGAIN)
        def _(b):
            first_row = pl.multiple_of(b * BLK, BLK)
            wide = mate_raw[pl.ds(first_row, BLK)].astype(jnp.float32)
            q_wide[...] = wide.reshape(BLK * heads, head_size)
            for h in range(heads):
                mate_q[h, pl.ds(first_row, BLK), :] = q_wide[
                    pl.ds(h, BLK, stride=heads), :
                ].astype(jnp.bfloat16)

        keys = n_ctx * blocks * BLK
        spread = (
            lax.broadcasted_iota(jnp.int32, (2 * BLK, keys), 1) // BLK
            == lax.broadcasted_iota(jnp.int32, (2 * BLK, keys), 0)
        )
        allowed = jnp.dot(
            allow_in[...].astype(jnp.bfloat16),
            jnp.where(spread, 1.0, 0.0).astype(jnp.bfloat16),
            preferred_element_type=jnp.float32,
        )
        key_at = lax.broadcasted_iota(jnp.int32, (BLK, keys), 1)
        query_row = lax.broadcasted_iota(jnp.int32, (BLK, keys), 0)
        for b in range(AGAIN):
            query_at = (c * blocks + first_again + b) * BLK + query_row
            mate_bias[b] = jnp.where(
                (allowed[b:b + 1] > 0.5) & (key_at <= query_at), 0.0, NEG_FILL
            )

        @pl.loop(0, AGAIN * 4)
        def _(i):
            b, quarter = i // 4, i % 4
            part = heads // 4
            from_row = pl.multiple_of(b * BLK, BLK)
            rows = mate_q[pl.ds(quarter * part, part), pl.ds(from_row, BLK), :]
            scores = lax.dot_general(
                rows.reshape(part * BLK, head_size), mate_kv[0].reshape(keys, head_size),
                (((1,), (1,)), ((), ())), preferred_element_type=jnp.float32,
            )
            scores = scores.reshape(part, BLK, keys) + mate_bias[b][None]
            scores = scores.reshape(part * BLK, keys)
            peak = jnp.max(scores, axis=-1, keepdims=True)
            weights = jnp.exp2((scores - peak) * exponent_scale)
            total = jnp.sum(weights, axis=-1, keepdims=True)
            mixed = jnp.dot(
                weights.astype(jnp.bfloat16), mate_kv[1].reshape(keys, head_size),
                preferred_element_type=jnp.float32,
            )
            mixed = (mixed / total).astype(jnp.bfloat16)
            to_row = pl.multiple_of((first_again + b) * BLK, BLK)
            for h in range(part):
                col = pl.multiple_of((quarter * part + h) * head_size, head_size)
                att_buf[mate, pl.ds(to_row, BLK), pl.ds(col, head_size)] = mixed[
                    h * BLK:(h + 1) * BLK
                ]

    depth = att_buf.shape[2]
    tile = 256
    n_tiles = out_ref.shape[1] // tile
    parts = OUT_PARTS
    part_rows = tokens // parts
    part_blocks = blocks // parts

    def product(owner, rows, cols):
        return jnp.dot(
            att_buf[owner, rows, :],
            w_buf[pl.ds(pl.multiple_of(owner * depth, depth), depth), cols],
            preferred_element_type=jnp.float32,
        )

    def add_product(owner):
        @pl.loop(0, n_tiles)
        def _(j):
            cols = pl.ds(pl.multiple_of(j * tile, tile), tile)
            acc[:, cols] += product(owner, slice(None), cols)

    far = last - z

    def add_in_full(chip_of):
        @pl.when(jnp.logical_not(at_end & (chip_of == far)))
        def _():
            add_product(chip_of)

    def w_ready(chip_of):
        for half in (0, 1):
            w_arrival(chip_of * CORES + (1 - core), half).wait_recv()

    w_pass(beside, 1, 1)
    w_pass(behind, 0, 2)

    @pl.when(in_middle)
    def _():
        @pl.loop(EARLY, blocks)
        def _(block):
            line_step(block, 2)

    @pl.when(at_end)
    def _():
        for distance in (1, 2):

            @pl.loop(0, blocks)
            def _(block, distance=distance):
                line_step(block, distance)

    for half in (0, 1):
        own_w[half].wait()
    for chip_of in (chip, beside, behind):
        w_ready(chip_of)
        add_in_full(chip_of)

    for half in (0, 1):
        w_pass(corner, half, 3)
    w_ready(corner)
    add_in_full(corner)

    @pl.when(at_end)
    def _():
        @pl.loop(0, parts)
        def _(p):
            @pl.loop(0, part_blocks)
            def _(b):
                line_step(p * part_blocks + b, last)

            rows = pl.ds(pl.multiple_of(p * part_rows, part_rows), part_rows)

            @pl.loop(0, n_tiles)
            def _(j):
                cols = pl.ds(pl.multiple_of(j * tile, tile), tile)
                total = acc[rows, cols] + product(far, rows, cols)
                out_ref[rows, cols] = total.astype(out_ref.dtype)


    @pl.when(in_middle)
    def _():
        out_ref[...] = acc[...].astype(out_ref.dtype)

    for part in (0, 1):
        own_across[part].wait_send()
    for half in (0, 1):
        own_w_across[half].wait_send()

    @pl.loop(1, n_chip)
    def _(step):
        for part in (0, 1):
            kv_across(c, part, step).wait_send()
        for half in (0, 1):
            w_across(c, half, step).wait_send()

    if square:
        for half in (0, 1):
            w_corner(half).wait_send()
            w_direct(beside, half, 1).wait_send()
            w_direct(behind, half, 2).wait_send()
            kv_corner(half).wait_send()
            kv_direct(beside, half, 1).wait_send()
            kv_direct(behind, half, 2).wait_send()
    else:

        @pl.loop(1, n_chip)
        def _(step):
            for half in (0, 1):
                w_direct(lax.rem(chip + step, n_chip), half, step).wait_send()
                kv_direct(lax.rem(chip + step, n_chip), half, step).wait_send()

    for distance in range(n_kvh):

        @pl.loop(0, blocks)
        def _(block, distance=distance):
            @pl.when((z >= distance) & (z < n_kvh - 1) & sent(block, z - distance, z + 1))
            def _():
                z_copy(z - distance, block, z_up, z + 1).wait_send()

            @pl.when((z + distance < n_kvh) & (z > 0) & sent(block, z + distance, z - 1))
            def _():
                z_copy(z + distance, block, z_down, z - 1).wait_send()

    @pl.when(in_middle)
    def _():
        for i in range(len(mate_pairs)):
            mate_copy(i).wait_send()

    @pl.when(at_end)
    def _():
        for part in (0, 1):
            mkv_corner(part).wait_send()
            mkv_direct(beside, part, 1).wait_send()
            mkv_direct(behind, part, 2).wait_send()
            for slot in range(n_chip):
                mkv_across(chip, part, slot).wait_send()


def solution(mesh):
    n_ctx, n_kvh = mesh.shape["ctx"], mesh.shape["kvh"]

    def on_device(queries, keys, values, vert_blocks, slash_offsets, out_weight):
        tokens, heads, head_size = queries.shape
        blocks = tokens // BLK
        n_slash, n_vert = slash_offsets.shape[1], vert_blocks.shape[1]
        n_slots = 1 + n_slash + n_vert
        n_slots += n_slots % 2
        w_rows, _, w_cols = out_weight.shape
        n_chip = n_ctx // CORES
        k = keys.reshape(blocks, BLK, head_size)
        v = values.reshape(blocks, BLK, head_size)
        dma = pltpu.SemaphoreType.DMA
        shared = [
            pltpu.VMEM((n_slots * BLK, head_size), jnp.bfloat16),
            pltpu.VMEM((n_slots * BLK, head_size), jnp.bfloat16),
            pltpu.VMEM((blocks, BLK, n_slots * BLK), jnp.float32),
            pltpu.VMEM((tokens, heads, head_size), jnp.bfloat16),
            pltpu.VMEM((BLK * heads, head_size), jnp.float32),
            pltpu.VMEM((heads, tokens, head_size), jnp.bfloat16),
        ]
        kv_buf = pltpu.VMEM((2, n_ctx * blocks, BLK, head_size), jnp.bfloat16)
        scratch = [
            kv_buf,
            pltpu.VMEM((n_ctx * w_rows, w_cols), jnp.bfloat16),
            pltpu.VMEM((n_kvh, tokens, heads * head_size), jnp.bfloat16),
            *shared,
            pltpu.VMEM((tokens, w_cols), jnp.float32),
        ]
        sems = [
            dma((5,)),
            dma((2, n_ctx)),
            dma((2, n_chip)),
            dma((2, n_chip)),
            dma((n_ctx, 2)),
            dma((n_chip, 2)),
            dma((n_chip, 2)),
            dma((n_kvh, blocks)),
            dma((n_kvh, blocks)),
            dma((n_kvh, blocks)),
        ]
        if n_chip == 4 and n_kvh == 4 and n_ctx * blocks <= 2 * BLK:
            body = functools.partial(line_kernel, n_ctx, n_kvh, n_slash, n_vert)
            out_space, limit = pltpu.VMEM, 50 * 2**20
            scratch += [
                kv_buf,
                pltpu.VMEM((AGAIN * BLK, heads, head_size), jnp.bfloat16),
                pltpu.VMEM((heads, AGAIN * BLK, head_size), jnp.bfloat16),
                pltpu.VMEM((8, 2 * BLK), jnp.float32),
                pltpu.VMEM((8, 2 * BLK), jnp.float32),
                pltpu.VMEM((AGAIN, BLK, n_ctx * tokens), jnp.float32),
                *sems,
                dma((4,)),
                dma((4,)),
                dma((2, n_ctx)),
                dma((2, n_chip)),
                dma((2, n_chip)),
            ]
        else:
            body = functools.partial(kernel, n_ctx, n_kvh, n_slash, n_vert)
            out_space, limit = pl.ANY, 56 * 2**20
            scratch += [pltpu.VMEM((tokens, w_cols), jnp.bfloat16), *sems, dma((2,))]
        return pl.pallas_call(
            body,
            out_shape=jax.ShapeDtypeStruct((tokens, w_cols), jnp.bfloat16),
            in_specs=[
                pl.BlockSpec(memory_space=pltpu.SMEM),
                pl.BlockSpec(memory_space=pltpu.SMEM),
                pl.BlockSpec(memory_space=pl.ANY),
                pl.BlockSpec(memory_space=pl.ANY),
                pl.BlockSpec(memory_space=pl.ANY),
                pl.BlockSpec(memory_space=pl.ANY),
            ],
            out_specs=pl.BlockSpec(memory_space=out_space),
            scratch_shapes=scratch,
            compiler_params=pltpu.CompilerParams(
                collective_id=0, has_side_effects=True, vmem_limit_bytes=limit
            ),
        )(
            *(
                pltpu.with_memory_space_constraint(x, pltpu.HBM)
                for x in (vert_blocks, slash_offsets, queries, k, v, out_weight.reshape(w_rows, w_cols))
            ),
        )

    return jax.shard_map(
        on_device,
        mesh=mesh,
        in_specs=(
            P("ctx", "kvh", None),
            P("ctx", "kvh", None),
            P("ctx", "kvh", None),
            P("kvh", None),
            P("kvh", None),
            P("ctx", "kvh", None),
        ),
        out_specs=P("ctx", "kvh"),
        check_vma=False,
    )
```

```python
import functools
import math

import jax
import jax.numpy as jnp
from jax import lax
from jax.experimental import pallas as pl
from jax.experimental.pallas import tpu as pltpu
from jax.sharding import PartitionSpec as P

BLK = 64
CORES = 2
NEG_FILL = -1e30
AGAIN = 3
EARLY = 5
OUT_PARTS = 3


def kernel(
    n_ctx, n_kvh, n_slash, n_vert,
    vert_ref, slash_ref, q_ref, k_ref, v_ref, w_ref, out_ref,
    kv_buf, w_buf, att_buf, kg, vg, bias, q_raw, q_wide, q_buf, acc, out_buf,
    local_sem, kv_recv, kv_send, kv_fwd, w_recv, w_send, w_fwd, z_recv, z_up, z_down, out_sem,
):
    c = lax.axis_index("ctx")
    z = lax.axis_index("kvh")
    n_chip = n_ctx // CORES
    chip, core = c // CORES, c % CORES
    sibling = chip * CORES + (1 - core)
    blocks = k_ref.shape[0]
    tokens, heads, head_size = q_ref.shape
    kv_refs = (k_ref, v_ref)
    w_rows = w_ref.shape[0]
    n_slots = kg.shape[0] // BLK

    def peer(step):
        return lax.rem(chip + step, n_chip) * CORES + core

    def sibling_source(step):
        return lax.rem(chip + n_chip - step, n_chip) * CORES + (1 - core)

    def kv_at(part, owner):
        return kv_buf.at[part, pl.ds(owner * blocks, blocks)]

    half_rows = w_rows // 2

    def w_at(owner, half):
        first = pl.multiple_of(owner * w_rows + half * half_rows, half_rows)
        return w_buf.at[pl.ds(first, half_rows)]

    def own_rows(half):
        return w_ref.at[pl.ds(half * half_rows, half_rows)]

    def push(src, dst, send_sem, recv_sem, to_ctx, to_z):
        return pltpu.make_async_remote_copy(
            src_ref=src, dst_ref=dst, send_sem=send_sem, recv_sem=recv_sem,
            device_id=(to_ctx, to_z), device_id_type=pl.DeviceIdType.MESH,
        )

    own_q = pltpu.make_async_copy(q_ref, q_raw, local_sem.at[2])
    own_q.start()
    own_w = [
        pltpu.make_async_copy(own_rows(half), w_at(c, half), local_sem.at[3 + half])
        for half in (0, 1)
    ]

    barrier = pltpu.get_barrier_semaphore()

    def greet(to_ctx, to_z):
        pl.semaphore_signal(
            barrier, inc=1, device_id=(to_ctx, to_z), device_id_type=pl.DeviceIdType.MESH
        )

    @pl.loop(1, n_chip)
    def _(step):
        greet(peer(step), z)

    greet(sibling, z)

    @pl.when(z > 0)
    def _():
        greet(c, z - 1)

    @pl.when(z < n_kvh - 1)
    def _():
        greet(c, z + 1)

    inner = jnp.where(z > 0, 1, 0) + jnp.where(z < n_kvh - 1, 1, 0)
    lane = lax.broadcasted_iota(jnp.int32, (BLK, 2 * BLK), 1)
    row = lax.broadcasted_iota(jnp.int32, (BLK, 2 * BLK), 0)

    @pl.loop(0, blocks)
    def _(block):
        place = c * blocks + block
        fills = [jnp.float32(0.0)]
        for j in range(n_slash):
            fills.append(jnp.where(place - slash_ref[0, j] >= 0, 0.0, NEG_FILL))
        for j in range(n_vert):
            gap = place - vert_ref[0, j]
            fill = jnp.where(gap > 0, 0.0, NEG_FILL)
            for k in range(n_slash):
                fill = jnp.where(gap == slash_ref[0, k], NEG_FILL, fill)
            fills.append(fill)
        while len(fills) < n_slots:
            fills.append(jnp.float32(NEG_FILL))
        for j in range(0, n_slots, 2):
            fill = jnp.where(lane < BLK, fills[j], fills[j + 1])
            if j == 0:
                fill = jnp.where((lane < BLK) & (lane > row), NEG_FILL, fill)
            bias[block, :, j * BLK:(j + 2) * BLK] = fill

    pl.semaphore_wait(barrier, n_chip + inner)

    square = n_chip == 4
    beside = (chip // 2) * 2 + (1 - chip % 2)
    behind = (1 - chip // 2) * 2 + chip % 2
    corner = n_chip - 1 - chip

    own_kv = [
        pltpu.make_async_copy(kv_refs[part], kv_at(part, c), local_sem.at[part]) for part in (0, 1)
    ]

    def kv_direct(to_chip, part, slot):
        return push(
            kv_refs[part], kv_at(part, c), kv_send.at[part, slot], kv_recv.at[part, c],
            to_chip * CORES + core, z,
        )

    def kv_arrival(owner, part):
        rows = kv_at(part, owner)
        return push(rows, rows, kv_send.at[part, 0], kv_recv.at[part, owner], c, z)

    def kv_across(owner, part, slot):
        rows = kv_at(part, owner)
        return push(rows, rows, kv_fwd.at[part, slot], kv_recv.at[part, owner], sibling, z)

    def kv_corner(part):
        from_chip, to_chip = (beside, behind) if part == 0 else (behind, beside)
        owner = from_chip * CORES + core
        rows = kv_at(part, owner)
        return push(
            rows, rows, kv_send.at[part, 0], kv_recv.at[part, owner], to_chip * CORES + core, z
        )

    def kv_pass(chip_from, part, slot):
        owner = chip_from * CORES + core
        kv_arrival(owner, part).wait_recv()
        kv_across(owner, part, slot).start()

    own_across = [
        push(kv_refs[part], kv_at(part, c), kv_fwd.at[part, 0], kv_recv.at[part, c], sibling, z)
        for part in (0, 1)
    ]

    if square:
        for first in (0, 1):
            kv_direct(beside, first, 1).start()
            kv_direct(behind, 1 - first, 2).start()
    else:

        @pl.loop(1, n_chip)
        def _(step):
            for part in (0, 1):
                kv_direct(lax.rem(chip + step, n_chip), part, step).start()

    for part in (0, 1):
        own_across[part].start()
        own_kv[part].start()

    for part in (0, 1):
        own_kv[part].wait()

    if square:
        for part, chip_from, slot in ((0, beside, 1), (1, behind, 2)):
            kv_arrival(chip_from * CORES + core, part).wait_recv()
            kv_corner(part).start()
            kv_across(chip_from * CORES + core, part, slot).start()

    own_q.wait()

    @pl.loop(0, blocks)
    def _(block):
        first_row = pl.multiple_of(block * BLK, BLK)
        wide = q_raw[pl.ds(first_row, BLK)].astype(jnp.float32)
        q_wide[...] = wide.reshape(BLK * heads, head_size)
        for h in range(heads):
            q_buf[h, pl.ds(first_row, BLK), :] = q_wide[
                pl.ds(h, BLK, stride=heads), :
            ].astype(jnp.bfloat16)

    if square:
        kv_pass(beside, 1, 1)
        kv_pass(behind, 0, 2)
        for part in (0, 1):
            kv_pass(corner, part, 3)
    else:

        @pl.loop(1, n_chip)
        def _(step):
            for part in (0, 1):
                kv_pass(lax.rem(chip + step, n_chip), part, step)

    def w_direct(to_chip, half, slot):
        return push(
            own_rows(half), w_at(c, half), w_send.at[slot, half], w_recv.at[c, half],
            to_chip * CORES + core, z,
        )

    def w_arrival(owner, half):
        return push(
            w_at(owner, half), w_at(owner, half), w_send.at[0, half], w_recv.at[owner, half], c, z
        )

    def w_across(owner, half, slot):
        return push(
            w_at(owner, half), w_at(owner, half), w_fwd.at[slot, half], w_recv.at[owner, half],
            sibling, z,
        )

    def w_corner(half):
        from_chip, to_chip = (beside, behind) if half == 0 else (behind, beside)
        owner = from_chip * CORES + core
        return push(
            w_at(owner, half), w_at(owner, half), w_send.at[0, half], w_recv.at[owner, half],
            to_chip * CORES + core, z,
        )

    if square:
        for first in (0, 1):
            w_direct(beside, first, 1).start()
            w_direct(behind, 1 - first, 2).start()
    else:

        @pl.loop(1, n_chip)
        def _(step):
            for half in (0, 1):
                w_direct(lax.rem(chip + step, n_chip), half, step).start()

    own_w_across = [
        push(own_rows(half), w_at(c, half), w_fwd.at[0, half], w_recv.at[c, half], sibling, z)
        for half in (0, 1)
    ]
    for half in (0, 1):
        own_w_across[half].start()
        own_w[half].start()

    def w_pass(chip_from, half, slot):
        owner = chip_from * CORES + core
        w_arrival(owner, half).wait_recv()
        w_across(owner, half, slot).start()

    @pl.loop(0, n_chip)
    def _(step):
        for part in (0, 1):
            kv_arrival(sibling_source(step), part).wait_recv()

    def z_copy(owner, block, sems, to_z):
        rows = att_buf.at[owner, pl.ds(pl.multiple_of(block * BLK, BLK), BLK)]
        return push(rows, rows, sems.at[owner, block], z_recv.at[owner, block], c, to_z)

    exponent_scale = math.log2(math.e) / math.sqrt(head_size)

    @pl.loop(0, blocks)
    def _(block):
        place = c * blocks + block
        picks = [place] + [jnp.maximum(place - slash_ref[0, j], 0) for j in range(n_slash)]
        picks += [vert_ref[0, j] for j in range(n_vert)]
        picks += [place] * (n_slots - len(picks))
        for j, pick in enumerate(picks):
            kg[j * BLK:(j + 1) * BLK, :] = kv_buf[0, pick]
            vg[j * BLK:(j + 1) * BLK, :] = kv_buf[1, pick]

        first_row = pl.multiple_of(block * BLK, BLK)
        part = heads // 2
        for half in range(2):
            rows = q_buf[half * part:(half + 1) * part, pl.ds(first_row, BLK), :]
            scores = lax.dot_general(
                rows.reshape(part * BLK, head_size), kg[...], (((1,), (1,)), ((), ())),
                preferred_element_type=jnp.float32,
            )
            scores = scores.reshape(part, BLK, n_slots * BLK) + bias[block][None]
            scores = scores.reshape(part * BLK, n_slots * BLK)
            peak = jnp.max(scores, axis=-1, keepdims=True)
            weights = jnp.exp2((scores - peak) * exponent_scale)
            total = jnp.sum(weights, axis=-1, keepdims=True)
            mixed = jnp.dot(
                weights.astype(jnp.bfloat16), vg[...], preferred_element_type=jnp.float32
            )
            mixed = (mixed / total).astype(jnp.bfloat16)
            for h in range(part):
                col = (half * part + h) * head_size
                att_buf[z, pl.ds(first_row, BLK), col:col + head_size] = mixed[
                    h * BLK:(h + 1) * BLK
                ]

        @pl.when(z < n_kvh - 1)
        def _():
            z_copy(z, block, z_up, z + 1).start()

        @pl.when(z > 0)
        def _():
            z_copy(z, block, z_down, z - 1).start()

    def line_step(block, distance):
        @pl.when(z >= distance)
        def _():
            z_copy(z - distance, block, z_up, z).wait_recv()

            if distance < n_kvh - 1:
                @pl.when(z < n_kvh - 1)
                def _():
                    z_copy(z - distance, block, z_up, z + 1).start()

        @pl.when(z + distance < n_kvh)
        def _():
            z_copy(z + distance, block, z_down, z).wait_recv()

            if distance < n_kvh - 1:
                @pl.when(z > 0)
                def _():
                    z_copy(z + distance, block, z_down, z - 1).start()

    if square:
        for half, chip_from, slot in ((0, beside, 1), (1, behind, 2)):
            w_arrival(chip_from * CORES + core, half).wait_recv()
            w_corner(half).start()
            w_across(chip_from * CORES + core, half, slot).start()

    for distance in range(1, n_kvh - 1):

        @pl.loop(0, blocks)
        def _(block, distance=distance):
            line_step(block, distance)

        if square and distance == 1:
            w_pass(beside, 1, 1)
            w_pass(behind, 0, 2)

    if square:
        for half in (0, 1):
            w_pass(corner, half, 3)
    else:

        @pl.loop(1, n_chip)
        def _(step):
            for half in (0, 1):
                w_pass(lax.rem(chip + step, n_chip), half, step)

    @pl.loop(0, n_chip)
    def _(step):
        for half in (0, 1):
            w_arrival(sibling_source(step), half).wait_recv()

    for half in (0, 1):
        own_w[half].wait()

    depth = att_buf.shape[2]
    tile = 256
    n_tiles = out_ref.shape[1] // tile
    parts = 2
    part_rows = tokens // parts
    part_blocks = blocks // parts

    def out_copy(p):
        rows = pl.ds(pl.multiple_of(p * part_rows, part_rows), part_rows)
        return pltpu.make_async_copy(out_buf.at[rows], out_ref.at[rows], out_sem.at[p])

    def product(owner, rows, cols):
        return jnp.dot(
            att_buf[owner, rows, :],
            w_buf[pl.ds(pl.multiple_of(owner * depth, depth), depth), cols],
            preferred_element_type=jnp.float32,
        )

    def add_product(owner):
        @pl.loop(0, n_tiles)
        def _(j):
            cols = pl.ds(pl.multiple_of(j * tile, tile), tile)
            acc[:, cols] += product(owner, slice(None), cols)

    @pl.loop(0, n_tiles)
    def _(j):
        cols = pl.ds(pl.multiple_of(j * tile, tile), tile)
        acc[:, cols] = product(z, slice(None), cols)

    for distance in range(1, n_kvh - 1):

        @pl.when(z >= distance)
        def _(distance=distance):
            add_product(z - distance)

        @pl.when(z + distance < n_kvh)
        def _(distance=distance):
            add_product(z + distance)

    last = n_kvh - 1
    at_end = (z == 0) | (z == last)
    far = last - z

    @pl.when(at_end)
    def _():
        @pl.loop(0, parts)
        def _(p):
            @pl.loop(0, part_blocks)
            def _(b):
                line_step(p * part_blocks + b, last)

            rows = pl.ds(pl.multiple_of(p * part_rows, part_rows), part_rows)

            @pl.loop(0, n_tiles)
            def _(j):
                cols = pl.ds(pl.multiple_of(j * tile, tile), tile)
                total = acc[rows, cols] + product(far, rows, cols)
                out_buf[rows, cols] = total.astype(out_ref.dtype)

            out_copy(p).start()

    @pl.when(jnp.logical_not(at_end))
    def _():
        out_buf[...] = acc[...].astype(out_ref.dtype)

        @pl.loop(0, parts)
        def _(p):
            out_copy(p).start()

    @pl.loop(0, parts)
    def _(p):
        out_copy(p).wait()

    for part in (0, 1):
        own_across[part].wait_send()
    for half in (0, 1):
        own_w_across[half].wait_send()

    @pl.loop(1, n_chip)
    def _(step):
        for part in (0, 1):
            kv_across(c, part, step).wait_send()
        for half in (0, 1):
            w_across(c, half, step).wait_send()

    if square:
        for half in (0, 1):
            w_corner(half).wait_send()
            w_direct(beside, half, 1).wait_send()
            w_direct(behind, half, 2).wait_send()
            kv_corner(half).wait_send()
            kv_direct(beside, half, 1).wait_send()
            kv_direct(behind, half, 2).wait_send()
    else:

        @pl.loop(1, n_chip)
        def _(step):
            for half in (0, 1):
                w_direct(lax.rem(chip + step, n_chip), half, step).wait_send()
                kv_direct(lax.rem(chip + step, n_chip), half, step).wait_send()

    for distance in range(n_kvh):

        @pl.loop(0, blocks)
        def _(block, distance=distance):
            @pl.when((z >= distance) & (z < n_kvh - 1))
            def _():
                z_copy(z - distance, block, z_up, z + 1).wait_send()

            @pl.when((z + distance < n_kvh) & (z > 0))
            def _():
                z_copy(z + distance, block, z_down, z - 1).wait_send()


def line_kernel(
    n_ctx, n_kvh, n_slash, n_vert,
    vert_ref, slash_ref, q_ref, k_ref, v_ref, w_ref, out_ref,
    kv_buf, w_buf, att_buf, kg, vg, bias, q_raw, q_wide, q_buf, acc,
    mate_kv, mate_raw, mate_q, allow_out, allow_in, mate_bias,
    local_sem, kv_recv, kv_send, kv_fwd, w_recv, w_send, w_fwd, z_recv, z_up, z_down,
    mate_recv, mate_send, mkv_recv, mkv_send, mkv_fwd,
):
    c = lax.axis_index("ctx")
    z = lax.axis_index("kvh")
    n_chip = n_ctx // CORES
    chip, core = c // CORES, c % CORES
    sibling = chip * CORES + (1 - core)
    blocks = k_ref.shape[0]
    tokens, heads, head_size = q_ref.shape
    kv_refs = (k_ref, v_ref)
    w_rows = w_ref.shape[0]
    n_slots = kg.shape[0] // BLK

    def peer(step):
        return lax.rem(chip + step, n_chip) * CORES + core

    def sibling_source(step):
        return lax.rem(chip + n_chip - step, n_chip) * CORES + (1 - core)

    def kv_at(part, owner):
        return kv_buf.at[part, pl.ds(owner * blocks, blocks)]

    half_rows = w_rows // 2

    def w_at(owner, half):
        first = pl.multiple_of(owner * w_rows + half * half_rows, half_rows)
        return w_buf.at[pl.ds(first, half_rows)]

    def own_rows(half):
        return w_ref.at[pl.ds(half * half_rows, half_rows)]

    def push(src, dst, send_sem, recv_sem, to_ctx, to_z):
        return pltpu.make_async_remote_copy(
            src_ref=src, dst_ref=dst, send_sem=send_sem, recv_sem=recv_sem,
            device_id=(to_ctx, to_z), device_id_type=pl.DeviceIdType.MESH,
        )

    own_q = pltpu.make_async_copy(q_ref, q_raw, local_sem.at[2])
    own_q.start()
    own_w = [
        pltpu.make_async_copy(own_rows(half), w_at(c, half), local_sem.at[3 + half])
        for half in (0, 1)
    ]

    barrier = pltpu.get_barrier_semaphore()

    def greet(to_ctx, to_z):
        pl.semaphore_signal(
            barrier, inc=1, device_id=(to_ctx, to_z), device_id_type=pl.DeviceIdType.MESH
        )

    @pl.loop(1, n_chip)
    def _(step):
        greet(peer(step), z)

    greet(sibling, z)

    @pl.when(z > 0)
    def _():
        greet(c, z - 1)

    @pl.when(z < n_kvh - 1)
    def _():
        greet(c, z + 1)

    last = n_kvh - 1
    at_end = (z == 0) | (z == last)
    in_middle = jnp.logical_not(at_end)
    mate = z + 1 - 2 * (z % 2)
    first_again = blocks - AGAIN

    inner = jnp.where(z > 0, 1, 0) + jnp.where(z < n_kvh - 1, 1, 0)
    lane = lax.broadcasted_iota(jnp.int32, (BLK, 2 * BLK), 1)
    row = lax.broadcasted_iota(jnp.int32, (BLK, 2 * BLK), 0)

    key_block = lax.broadcasted_iota(jnp.int32, (8, 2 * BLK), 1)
    again_place = c * blocks + first_again + lax.broadcasted_iota(jnp.int32, (8, 2 * BLK), 0)
    kept = key_block == again_place
    for j in range(n_slash):
        kept = kept | (again_place - key_block == slash_ref[0, j])
    for j in range(n_vert):
        kept = kept | ((key_block == vert_ref[0, j]) & (key_block < again_place))
    allow_out[...] = jnp.where(kept, 1.0, 0.0)

    pl.semaphore_wait(barrier, n_chip + inner)

    square = n_chip == 4
    beside = (chip // 2) * 2 + (1 - chip % 2)
    behind = (1 - chip // 2) * 2 + chip % 2
    corner = n_chip - 1 - chip

    mate_pairs = (
        (k_ref, mate_kv.at[0, pl.ds(c * blocks, blocks)]),
        (v_ref, mate_kv.at[1, pl.ds(c * blocks, blocks)]),
        (allow_out, allow_in),
        (q_ref.at[pl.ds(first_again * BLK, AGAIN * BLK)], mate_raw),
    )

    def mate_copy(i):
        src, dst = mate_pairs[i]
        return push(src, dst, mate_send.at[i], mate_recv.at[i], c, mate)

    @pl.when(in_middle)
    def _():
        for i in range(len(mate_pairs)):
            mate_copy(i).start()

    own_kv = [
        pltpu.make_async_copy(kv_refs[part], kv_at(part, c), local_sem.at[part]) for part in (0, 1)
    ]

    def kv_direct(to_chip, part, slot):
        return push(
            kv_refs[part], kv_at(part, c), kv_send.at[part, slot], kv_recv.at[part, c],
            to_chip * CORES + core, z,
        )

    def kv_arrival(owner, part):
        rows = kv_at(part, owner)
        return push(rows, rows, kv_send.at[part, 0], kv_recv.at[part, owner], c, z)

    def kv_across(owner, part, slot):
        rows = kv_at(part, owner)
        return push(rows, rows, kv_fwd.at[part, slot], kv_recv.at[part, owner], sibling, z)

    def kv_corner(part):
        from_chip, to_chip = (beside, behind) if part == 0 else (behind, beside)
        owner = from_chip * CORES + core
        rows = kv_at(part, owner)
        return push(
            rows, rows, kv_send.at[part, 0], kv_recv.at[part, owner], to_chip * CORES + core, z
        )

    def kv_pass(chip_from, part, slot):
        owner = chip_from * CORES + core
        kv_arrival(owner, part).wait_recv()
        kv_across(owner, part, slot).start()

    own_across = [
        push(kv_refs[part], kv_at(part, c), kv_fwd.at[part, 0], kv_recv.at[part, c], sibling, z)
        for part in (0, 1)
    ]

    if square:
        for first in (0, 1):
            kv_direct(beside, first, 1).start()
            kv_direct(behind, 1 - first, 2).start()
    else:

        @pl.loop(1, n_chip)
        def _(step):
            for part in (0, 1):
                kv_direct(lax.rem(chip + step, n_chip), part, step).start()

    for part in (0, 1):
        own_across[part].start()
        own_kv[part].start()

    @pl.loop(0, blocks)
    def _(block):
        place = c * blocks + block
        fills = [jnp.float32(0.0)]
        for j in range(n_slash):
            fills.append(jnp.where(place - slash_ref[0, j] >= 0, 0.0, NEG_FILL))
        for j in range(n_vert):
            gap = place - vert_ref[0, j]
            fill = jnp.where(gap > 0, 0.0, NEG_FILL)
            for k in range(n_slash):
                fill = jnp.where(gap == slash_ref[0, k], NEG_FILL, fill)
            fills.append(fill)
        while len(fills) < n_slots:
            fills.append(jnp.float32(NEG_FILL))
        for j in range(0, n_slots, 2):
            fill = jnp.where(lane < BLK, fills[j], fills[j + 1])
            if j == 0:
                fill = jnp.where((lane < BLK) & (lane > row), NEG_FILL, fill)
            bias[block, :, j * BLK:(j + 2) * BLK] = fill

    for part in (0, 1):
        own_kv[part].wait()

    if square:
        for part, chip_from, slot in ((0, beside, 1), (1, behind, 2)):
            kv_arrival(chip_from * CORES + core, part).wait_recv()
            kv_corner(part).start()
            kv_across(chip_from * CORES + core, part, slot).start()

    own_q.wait()

    @pl.loop(0, blocks)
    def _(block):
        first_row = pl.multiple_of(block * BLK, BLK)
        wide = q_raw[pl.ds(first_row, BLK)].astype(jnp.float32)
        q_wide[...] = wide.reshape(BLK * heads, head_size)
        for h in range(heads):
            q_buf[h, pl.ds(first_row, BLK), :] = q_wide[
                pl.ds(h, BLK, stride=heads), :
            ].astype(jnp.bfloat16)

    if square:
        kv_pass(beside, 1, 1)
        kv_pass(behind, 0, 2)
        for part in (0, 1):
            kv_pass(corner, part, 3)
    else:

        @pl.loop(1, n_chip)
        def _(step):
            for part in (0, 1):
                kv_pass(lax.rem(chip + step, n_chip), part, step)

    def mkv_at(part, chip_of, core_of):
        return mate_kv.at[part, pl.ds((chip_of * CORES + core_of) * blocks, blocks)]

    def mkv_copy(chip_of, part, sem, to_ctx):
        rows = mkv_at(part, chip_of, core)
        return push(rows, rows, sem, mkv_recv.at[part, chip_of * CORES + core], to_ctx, z)

    def mkv_direct(to_chip, part, slot):
        return mkv_copy(chip, part, mkv_send.at[part, slot], to_chip * CORES + core)

    def mkv_across(chip_of, part, slot):
        return mkv_copy(chip_of, part, mkv_fwd.at[part, slot], sibling)

    def mkv_corner(part):
        from_chip, to_chip = (beside, behind) if part == 0 else (behind, beside)
        return mkv_copy(from_chip, part, mkv_send.at[part, 0], to_chip * CORES + core)

    def mkv_arrival(chip_of, core_of, part):
        rows = mkv_at(part, chip_of, core_of)
        return push(
            rows, rows, mkv_send.at[part, 0], mkv_recv.at[part, chip_of * CORES + core_of],
            sibling, z,
        )

    @pl.when(at_end)
    def _():
        for i in (0, 1):
            mate_copy(i).wait_recv()
        for first in (0, 1):
            mkv_direct(beside, first, 1).start()
            mkv_direct(behind, 1 - first, 2).start()
        for part in (0, 1):
            mkv_across(chip, part, 0).start()

    def w_direct(to_chip, half, slot):
        return push(
            own_rows(half), w_at(c, half), w_send.at[slot, half], w_recv.at[c, half],
            to_chip * CORES + core, z,
        )

    def w_arrival(owner, half):
        return push(
            w_at(owner, half), w_at(owner, half), w_send.at[0, half], w_recv.at[owner, half], c, z
        )

    def w_across(owner, half, slot):
        return push(
            w_at(owner, half), w_at(owner, half), w_fwd.at[slot, half], w_recv.at[owner, half],
            sibling, z,
        )

    def w_corner(half):
        from_chip, to_chip = (beside, behind) if half == 0 else (behind, beside)
        owner = from_chip * CORES + core
        return push(
            w_at(owner, half), w_at(owner, half), w_send.at[0, half], w_recv.at[owner, half],
            to_chip * CORES + core, z,
        )

    w_direct(beside, 0, 1).start()
    w_direct(behind, 1, 2).start()

    own_w_across = [
        push(own_rows(half), w_at(c, half), w_fwd.at[0, half], w_recv.at[c, half], sibling, z)
        for half in (0, 1)
    ]
    for half in (0, 1):
        own_w_across[half].start()
        own_w[half].start()

    def w_pass(chip_from, half, slot):
        owner = chip_from * CORES + core
        w_arrival(owner, half).wait_recv()
        w_across(owner, half, slot).start()

    @pl.loop(0, n_chip)
    def _(step):
        for part in (0, 1):
            kv_arrival(sibling_source(step), part).wait_recv()

    def z_copy(owner, block, sems, to_z):
        rows = att_buf.at[owner, pl.ds(pl.multiple_of(block * BLK, BLK), BLK)]
        return push(rows, rows, sems.at[owner, block], z_recv.at[owner, block], c, to_z)

    def sent(block, owner, to_z):
        ends = ((owner == 1) & (to_z == 0)) | ((owner == last - 1) & (to_z == last))
        return jnp.logical_not(ends & (block >= first_again))

    def line_step(block, distance):
        @pl.when((z >= distance) & sent(block, z - distance, z))
        def _():
            z_copy(z - distance, block, z_up, z).wait_recv()

            if distance < n_kvh - 1:
                @pl.when(z < n_kvh - 1)
                def _():
                    z_copy(z - distance, block, z_up, z + 1).start()

        @pl.when((z + distance < n_kvh) & sent(block, z + distance, z))
        def _():
            z_copy(z + distance, block, z_down, z).wait_recv()

            if distance < n_kvh - 1:
                @pl.when(z > 0)
                def _():
                    z_copy(z + distance, block, z_down, z - 1).start()

    exponent_scale = math.log2(math.e) / math.sqrt(head_size)

    @pl.loop(0, blocks)
    def _(block):
        place = c * blocks + block
        picks = [place] + [jnp.maximum(place - slash_ref[0, j], 0) for j in range(n_slash)]
        picks += [vert_ref[0, j] for j in range(n_vert)]
        picks += [place] * (n_slots - len(picks))
        for j, pick in enumerate(picks):
            kg[j * BLK:(j + 1) * BLK, :] = kv_buf[0, pick]
            vg[j * BLK:(j + 1) * BLK, :] = kv_buf[1, pick]

        first_row = pl.multiple_of(block * BLK, BLK)
        part = heads // 2
        for half in range(2):
            rows = q_buf[half * part:(half + 1) * part, pl.ds(first_row, BLK), :]
            scores = lax.dot_general(
                rows.reshape(part * BLK, head_size), kg[...], (((1,), (1,)), ((), ())),
                preferred_element_type=jnp.float32,
            )
            scores = scores.reshape(part, BLK, n_slots * BLK) + bias[block][None]
            scores = scores.reshape(part * BLK, n_slots * BLK)
            peak = jnp.max(scores, axis=-1, keepdims=True)
            weights = jnp.exp2((scores - peak) * exponent_scale)
            total = jnp.sum(weights, axis=-1, keepdims=True)
            mixed = jnp.dot(
                weights.astype(jnp.bfloat16), vg[...], preferred_element_type=jnp.float32
            )
            mixed = (mixed / total).astype(jnp.bfloat16)
            for h in range(part):
                col = (half * part + h) * head_size
                att_buf[z, pl.ds(first_row, BLK), col:col + head_size] = mixed[
                    h * BLK:(h + 1) * BLK
                ]

        @pl.when((z < n_kvh - 1) & sent(block, z, z + 1))
        def _():
            z_copy(z, block, z_up, z + 1).start()

        @pl.when((z > 0) & sent(block, z, z - 1))
        def _():
            z_copy(z, block, z_down, z - 1).start()

        @pl.when(block == 2)
        def _():
            @pl.when(at_end)
            def _():
                for part, chip_from, slot in ((0, beside, 1), (1, behind, 2)):
                    mkv_arrival(chip_from, core, part).wait_recv()
                    mkv_corner(part).start()
                    mkv_across(chip_from, part, slot).start()

            w_direct(beside, 1, 1).start()
            w_direct(behind, 0, 2).start()

        @pl.when(in_middle & (block >= EARLY))
        def _():
            line_step(block - EARLY, 1)

    for half, chip_from, slot in ((0, beside, 1), (1, behind, 2)):
        w_arrival(chip_from * CORES + core, half).wait_recv()
        w_corner(half).start()
        w_across(chip_from * CORES + core, half, slot).start()

    acc[...] = jnp.zeros_like(acc)

    @pl.when(in_middle)
    def _():
        @pl.loop(blocks - EARLY, min(EARLY + 1, blocks))
        def _(block):
            line_step(block, 1)

        @pl.loop(0, max(blocks - 1 - EARLY, 0))
        def _(block):
            line_step(block, 2)
            line_step(EARLY + 1 + block, 1)

    @pl.when(at_end)
    def _():
        mkv_pass = ((beside, 1, 1), (behind, 0, 2), (corner, 0, 3), (corner, 1, 3))
        for chip_from, part, slot in mkv_pass:
            mkv_arrival(chip_from, core, part).wait_recv()
            mkv_across(chip_from, part, slot).start()
        for i in (2, 3):
            mate_copy(i).wait_recv()

        @pl.loop(0, n_chip)
        def _(chip_of):
            for part in (0, 1):
                mkv_arrival(chip_of, 1 - core, part).wait_recv()

        @pl.loop(0, AGAIN)
        def _(b):
            first_row = pl.multiple_of(b * BLK, BLK)
            wide = mate_raw[pl.ds(first_row, BLK)].astype(jnp.float32)
            q_wide[...] = wide.reshape(BLK * heads, head_size)
            for h in range(heads):
                mate_q[h, pl.ds(first_row, BLK), :] = q_wide[
                    pl.ds(h, BLK, stride=heads), :
                ].astype(jnp.bfloat16)

        keys = n_ctx * blocks * BLK
        spread = (
            lax.broadcasted_iota(jnp.int32, (2 * BLK, keys), 1) // BLK
            == lax.broadcasted_iota(jnp.int32, (2 * BLK, keys), 0)
        )
        allowed = jnp.dot(
            allow_in[...].astype(jnp.bfloat16),
            jnp.where(spread, 1.0, 0.0).astype(jnp.bfloat16),
            preferred_element_type=jnp.float32,
        )
        key_at = lax.broadcasted_iota(jnp.int32, (BLK, keys), 1)
        query_row = lax.broadcasted_iota(jnp.int32, (BLK, keys), 0)
        for b in range(AGAIN):
            query_at = (c * blocks + first_again + b) * BLK + query_row
            mate_bias[b] = jnp.where(
                (allowed[b:b + 1] > 0.5) & (key_at <= query_at), 0.0, NEG_FILL
            )

        @pl.loop(0, AGAIN * 4)
        def _(i):
            b, quarter = i // 4, i % 4
            part = heads // 4
            from_row = pl.multiple_of(b * BLK, BLK)
            rows = mate_q[pl.ds(quarter * part, part), pl.ds(from_row, BLK), :]
            scores = lax.dot_general(
                rows.reshape(part * BLK, head_size), mate_kv[0].reshape(keys, head_size),
                (((1,), (1,)), ((), ())), preferred_element_type=jnp.float32,
            )
            scores = scores.reshape(part, BLK, keys) + mate_bias[b][None]
            scores = scores.reshape(part * BLK, keys)
            peak = jnp.max(scores, axis=-1, keepdims=True)
            weights = jnp.exp2((scores - peak) * exponent_scale)
            total = jnp.sum(weights, axis=-1, keepdims=True)
            mixed = jnp.dot(
                weights.astype(jnp.bfloat16), mate_kv[1].reshape(keys, head_size),
                preferred_element_type=jnp.float32,
            )
            mixed = (mixed / total).astype(jnp.bfloat16)
            to_row = pl.multiple_of((first_again + b) * BLK, BLK)
            for h in range(part):
                col = pl.multiple_of((quarter * part + h) * head_size, head_size)
                att_buf[mate, pl.ds(to_row, BLK), pl.ds(col, head_size)] = mixed[
                    h * BLK:(h + 1) * BLK
                ]

    depth = att_buf.shape[2]
    tile = 256
    n_tiles = out_ref.shape[1] // tile
    parts = OUT_PARTS
    part_rows = tokens // parts
    part_blocks = blocks // parts

    def product(owner, rows, cols):
        return jnp.dot(
            att_buf[owner, rows, :],
            w_buf[pl.ds(pl.multiple_of(owner * depth, depth), depth), cols],
            preferred_element_type=jnp.float32,
        )

    def add_product(owner):
        @pl.loop(0, n_tiles)
        def _(j):
            cols = pl.ds(pl.multiple_of(j * tile, tile), tile)
            acc[:, cols] += product(owner, slice(None), cols)

    far = last - z

    def add_in_full(chip_of):
        @pl.when(jnp.logical_not(at_end & (chip_of == far)))
        def _():
            add_product(chip_of)

    def w_ready(chip_of):
        for half in (0, 1):
            w_arrival(chip_of * CORES + (1 - core), half).wait_recv()

    w_pass(beside, 1, 1)
    w_pass(behind, 0, 2)

    @pl.when(in_middle)
    def _():
        @pl.loop(max(blocks - 1 - EARLY, 0), blocks)
        def _(block):
            line_step(block, 2)

    @pl.when(at_end)
    def _():
        for distance in (1, 2):

            @pl.loop(0, blocks)
            def _(block, distance=distance):
                line_step(block, distance)

    for half in (0, 1):
        own_w[half].wait()
    for chip_of in (chip, beside, behind):
        w_ready(chip_of)
        add_in_full(chip_of)

    for half in (0, 1):
        w_pass(corner, half, 3)
    w_ready(corner)
    add_in_full(corner)

    @pl.when(in_middle)
    def _():
        out_ref[...] = acc[...].astype(out_ref.dtype)

    for part in (0, 1):
        own_across[part].wait_send()
    for half in (0, 1):
        own_w_across[half].wait_send()

    @pl.loop(1, n_chip)
    def _(step):
        for part in (0, 1):
            kv_across(c, part, step).wait_send()
        for half in (0, 1):
            w_across(c, half, step).wait_send()

    if square:
        for half in (0, 1):
            w_corner(half).wait_send()
            w_direct(beside, half, 1).wait_send()
            w_direct(behind, half, 2).wait_send()
            kv_corner(half).wait_send()
            kv_direct(beside, half, 1).wait_send()
            kv_direct(behind, half, 2).wait_send()
    else:

        @pl.loop(1, n_chip)
        def _(step):
            for half in (0, 1):
                w_direct(lax.rem(chip + step, n_chip), half, step).wait_send()
                kv_direct(lax.rem(chip + step, n_chip), half, step).wait_send()

    for distance in range(n_kvh):

        @pl.loop(0, blocks)
        def _(block, distance=distance):
            @pl.when((z >= distance) & (z < n_kvh - 1) & sent(block, z - distance, z + 1))
            def _():
                z_copy(z - distance, block, z_up, z + 1).wait_send()

            @pl.when((z + distance < n_kvh) & (z > 0) & sent(block, z + distance, z - 1))
            def _():
                z_copy(z + distance, block, z_down, z - 1).wait_send()

    @pl.when(in_middle)
    def _():
        for i in range(len(mate_pairs)):
            mate_copy(i).wait_send()

    @pl.when(at_end)
    def _():
        for part in (0, 1):
            mkv_corner(part).wait_send()
            mkv_direct(beside, part, 1).wait_send()
            mkv_direct(behind, part, 2).wait_send()
            for slot in range(n_chip):
                mkv_across(chip, part, slot).wait_send()

    @pl.when(at_end)
    def _():
        @pl.loop(0, parts)
        def _(p):
            @pl.loop(0, part_blocks)
            def _(b):
                line_step(p * part_blocks + b, last)

            rows = pl.ds(pl.multiple_of(p * part_rows, part_rows), part_rows)

            @pl.loop(0, n_tiles)
            def _(j):
                cols = pl.ds(pl.multiple_of(j * tile, tile), tile)
                total = acc[rows, cols] + product(far, rows, cols)
                out_ref[rows, cols] = total.astype(out_ref.dtype)


def solution(mesh):
    n_ctx, n_kvh = mesh.shape["ctx"], mesh.shape["kvh"]

    def on_device(queries, keys, values, vert_blocks, slash_offsets, out_weight):
        tokens, heads, head_size = queries.shape
        blocks = tokens // BLK
        n_slash, n_vert = slash_offsets.shape[1], vert_blocks.shape[1]
        n_slots = 1 + n_slash + n_vert
        n_slots += n_slots % 2
        w_rows, _, w_cols = out_weight.shape
        n_chip = n_ctx // CORES
        k = keys.reshape(blocks, BLK, head_size)
        v = values.reshape(blocks, BLK, head_size)
        dma = pltpu.SemaphoreType.DMA
        shared = [
            pltpu.VMEM((n_slots * BLK, head_size), jnp.bfloat16),
            pltpu.VMEM((n_slots * BLK, head_size), jnp.bfloat16),
            pltpu.VMEM((blocks, BLK, n_slots * BLK), jnp.float32),
            pltpu.VMEM((tokens, heads, head_size), jnp.bfloat16),
            pltpu.VMEM((BLK * heads, head_size), jnp.float32),
            pltpu.VMEM((heads, tokens, head_size), jnp.bfloat16),
        ]
        kv_buf = pltpu.VMEM((2, n_ctx * blocks, BLK, head_size), jnp.bfloat16)
        scratch = [
            kv_buf,
            pltpu.VMEM((n_ctx * w_rows, w_cols), jnp.bfloat16),
            pltpu.VMEM((n_kvh, tokens, heads * head_size), jnp.bfloat16),
            *shared,
            pltpu.VMEM((tokens, w_cols), jnp.float32),
        ]
        sems = [
            dma((5,)),
            dma((2, n_ctx)),
            dma((2, n_chip)),
            dma((2, n_chip)),
            dma((n_ctx, 2)),
            dma((n_chip, 2)),
            dma((n_chip, 2)),
            dma((n_kvh, blocks)),
            dma((n_kvh, blocks)),
            dma((n_kvh, blocks)),
        ]
        if n_chip == 4 and n_kvh == 4 and n_ctx * blocks <= 2 * BLK:
            body = functools.partial(line_kernel, n_ctx, n_kvh, n_slash, n_vert)
            out_space, limit = pltpu.VMEM, 50 * 2**20
            scratch += [
                kv_buf,
                pltpu.VMEM((AGAIN * BLK, heads, head_size), jnp.bfloat16),
                pltpu.VMEM((heads, AGAIN * BLK, head_size), jnp.bfloat16),
                pltpu.VMEM((8, 2 * BLK), jnp.float32),
                pltpu.VMEM((8, 2 * BLK), jnp.float32),
                pltpu.VMEM((AGAIN, BLK, n_ctx * tokens), jnp.float32),
                *sems,
                dma((4,)),
                dma((4,)),
                dma((2, n_ctx)),
                dma((2, n_chip)),
                dma((2, n_chip)),
            ]
        else:
            body = functools.partial(kernel, n_ctx, n_kvh, n_slash, n_vert)
            out_space, limit = pl.ANY, 56 * 2**20
            scratch += [pltpu.VMEM((tokens, w_cols), jnp.bfloat16), *sems, dma((2,))]
        return pl.pallas_call(
            body,
            out_shape=jax.ShapeDtypeStruct((tokens, w_cols), jnp.bfloat16),
            in_specs=[
                pl.BlockSpec(memory_space=pltpu.SMEM),
                pl.BlockSpec(memory_space=pltpu.SMEM),
                pl.BlockSpec(memory_space=pl.ANY),
                pl.BlockSpec(memory_space=pl.ANY),
                pl.BlockSpec(memory_space=pl.ANY),
                pl.BlockSpec(memory_space=pl.ANY),
            ],
            out_specs=pl.BlockSpec(memory_space=out_space),
            scratch_shapes=scratch,
            compiler_params=pltpu.CompilerParams(
                collective_id=0, has_side_effects=True, vmem_limit_bytes=limit
            ),
        )(
            *(
                pltpu.with_memory_space_constraint(x, pltpu.HBM)
                for x in (vert_blocks, slash_offsets, queries, k, v, out_weight.reshape(w_rows, w_cols))
            ),
        )

    return jax.shard_map(
        on_device,
        mesh=mesh,
        in_specs=(
            P("ctx", "kvh", None),
            P("ctx", "kvh", None),
            P("ctx", "kvh", None),
            P("kvh", None),
            P("kvh", None),
            P("ctx", "kvh", None),
        ),
        out_specs=P("ctx", "kvh"),
        check_vma=False,
    )
```

```python
import functools
import math

import jax
import jax.numpy as jnp
from jax import lax
from jax.experimental import pallas as pl
from jax.experimental.pallas import tpu as pltpu
from jax.sharding import PartitionSpec as P

BLK = 64
CORES = 2
NEG_FILL = -1e30
AGAIN = 3
EARLY = 5
OUT_PARTS = 3


def kernel(
    n_ctx, n_kvh, n_slash, n_vert,
    vert_ref, slash_ref, q_ref, k_ref, v_ref, w_ref, out_ref,
    kv_buf, w_buf, att_buf, kg, vg, bias, q_raw, q_wide, q_buf, acc, out_buf,
    local_sem, kv_recv, kv_send, kv_fwd, w_recv, w_send, w_fwd, z_recv, z_up, z_down, out_sem,
):
    c = lax.axis_index("ctx")
    z = lax.axis_index("kvh")
    n_chip = n_ctx // CORES
    chip, core = c // CORES, c % CORES
    sibling = chip * CORES + (1 - core)
    blocks = k_ref.shape[0]
    tokens, heads, head_size = q_ref.shape
    kv_refs = (k_ref, v_ref)
    w_rows = w_ref.shape[0]
    n_slots = kg.shape[0] // BLK

    def peer(step):
        return lax.rem(chip + step, n_chip) * CORES + core

    def sibling_source(step):
        return lax.rem(chip + n_chip - step, n_chip) * CORES + (1 - core)

    def kv_at(part, owner):
        return kv_buf.at[part, pl.ds(owner * blocks, blocks)]

    half_rows = w_rows // 2

    def w_at(owner, half):
        first = pl.multiple_of(owner * w_rows + half * half_rows, half_rows)
        return w_buf.at[pl.ds(first, half_rows)]

    def own_rows(half):
        return w_ref.at[pl.ds(half * half_rows, half_rows)]

    def push(src, dst, send_sem, recv_sem, to_ctx, to_z):
        return pltpu.make_async_remote_copy(
            src_ref=src, dst_ref=dst, send_sem=send_sem, recv_sem=recv_sem,
            device_id=(to_ctx, to_z), device_id_type=pl.DeviceIdType.MESH,
        )

    own_q = pltpu.make_async_copy(q_ref, q_raw, local_sem.at[2])
    own_q.start()
    own_w = [
        pltpu.make_async_copy(own_rows(half), w_at(c, half), local_sem.at[3 + half])
        for half in (0, 1)
    ]

    barrier = pltpu.get_barrier_semaphore()

    def greet(to_ctx, to_z):
        pl.semaphore_signal(
            barrier, inc=1, device_id=(to_ctx, to_z), device_id_type=pl.DeviceIdType.MESH
        )

    @pl.loop(1, n_chip)
    def _(step):
        greet(peer(step), z)

    greet(sibling, z)

    @pl.when(z > 0)
    def _():
        greet(c, z - 1)

    @pl.when(z < n_kvh - 1)
    def _():
        greet(c, z + 1)

    inner = jnp.where(z > 0, 1, 0) + jnp.where(z < n_kvh - 1, 1, 0)
    lane = lax.broadcasted_iota(jnp.int32, (BLK, 2 * BLK), 1)
    row = lax.broadcasted_iota(jnp.int32, (BLK, 2 * BLK), 0)

    @pl.loop(0, blocks)
    def _(block):
        place = c * blocks + block
        fills = [jnp.float32(0.0)]
        for j in range(n_slash):
            fills.append(jnp.where(place - slash_ref[0, j] >= 0, 0.0, NEG_FILL))
        for j in range(n_vert):
            gap = place - vert_ref[0, j]
            fill = jnp.where(gap > 0, 0.0, NEG_FILL)
            for k in range(n_slash):
                fill = jnp.where(gap == slash_ref[0, k], NEG_FILL, fill)
            fills.append(fill)
        while len(fills) < n_slots:
            fills.append(jnp.float32(NEG_FILL))
        for j in range(0, n_slots, 2):
            fill = jnp.where(lane < BLK, fills[j], fills[j + 1])
            if j == 0:
                fill = jnp.where((lane < BLK) & (lane > row), NEG_FILL, fill)
            bias[block, :, j * BLK:(j + 2) * BLK] = fill

    pl.semaphore_wait(barrier, n_chip + inner)

    square = n_chip == 4
    beside = (chip // 2) * 2 + (1 - chip % 2)
    behind = (1 - chip // 2) * 2 + chip % 2
    corner = n_chip - 1 - chip

    own_kv = [
        pltpu.make_async_copy(kv_refs[part], kv_at(part, c), local_sem.at[part]) for part in (0, 1)
    ]

    def kv_direct(to_chip, part, slot):
        return push(
            kv_refs[part], kv_at(part, c), kv_send.at[part, slot], kv_recv.at[part, c],
            to_chip * CORES + core, z,
        )

    def kv_arrival(owner, part):
        rows = kv_at(part, owner)
        return push(rows, rows, kv_send.at[part, 0], kv_recv.at[part, owner], c, z)

    def kv_across(owner, part, slot):
        rows = kv_at(part, owner)
        return push(rows, rows, kv_fwd.at[part, slot], kv_recv.at[part, owner], sibling, z)

    def kv_corner(part):
        from_chip, to_chip = (beside, behind) if part == 0 else (behind, beside)
        owner = from_chip * CORES + core
        rows = kv_at(part, owner)
        return push(
            rows, rows, kv_send.at[part, 0], kv_recv.at[part, owner], to_chip * CORES + core, z
        )

    def kv_pass(chip_from, part, slot):
        owner = chip_from * CORES + core
        kv_arrival(owner, part).wait_recv()
        kv_across(owner, part, slot).start()

    own_across = [
        push(kv_refs[part], kv_at(part, c), kv_fwd.at[part, 0], kv_recv.at[part, c], sibling, z)
        for part in (0, 1)
    ]

    if square:
        for first in (0, 1):
            kv_direct(beside, first, 1).start()
            kv_direct(behind, 1 - first, 2).start()
    else:

        @pl.loop(1, n_chip)
        def _(step):
            for part in (0, 1):
                kv_direct(lax.rem(chip + step, n_chip), part, step).start()

    for part in (0, 1):
        own_across[part].start()
        own_kv[part].start()

    for part in (0, 1):
        own_kv[part].wait()

    if square:
        for part, chip_from, slot in ((0, beside, 1), (1, behind, 2)):
            kv_arrival(chip_from * CORES + core, part).wait_recv()
            kv_corner(part).start()
            kv_across(chip_from * CORES + core, part, slot).start()

    own_q.wait()

    @pl.loop(0, blocks)
    def _(block):
        first_row = pl.multiple_of(block * BLK, BLK)
        wide = q_raw[pl.ds(first_row, BLK)].astype(jnp.float32)
        q_wide[...] = wide.reshape(BLK * heads, head_size)
        for h in range(heads):
            q_buf[h, pl.ds(first_row, BLK), :] = q_wide[
                pl.ds(h, BLK, stride=heads), :
            ].astype(jnp.bfloat16)

    if square:
        kv_pass(beside, 1, 1)
        kv_pass(behind, 0, 2)
        for part in (0, 1):
            kv_pass(corner, part, 3)
    else:

        @pl.loop(1, n_chip)
        def _(step):
            for part in (0, 1):
                kv_pass(lax.rem(chip + step, n_chip), part, step)

    def w_direct(to_chip, half, slot):
        return push(
            own_rows(half), w_at(c, half), w_send.at[slot, half], w_recv.at[c, half],
            to_chip * CORES + core, z,
        )

    def w_arrival(owner, half):
        return push(
            w_at(owner, half), w_at(owner, half), w_send.at[0, half], w_recv.at[owner, half], c, z
        )

    def w_across(owner, half, slot):
        return push(
            w_at(owner, half), w_at(owner, half), w_fwd.at[slot, half], w_recv.at[owner, half],
            sibling, z,
        )

    def w_corner(half):
        from_chip, to_chip = (beside, behind) if half == 0 else (behind, beside)
        owner = from_chip * CORES + core
        return push(
            w_at(owner, half), w_at(owner, half), w_send.at[0, half], w_recv.at[owner, half],
            to_chip * CORES + core, z,
        )

    if square:
        for first in (0, 1):
            w_direct(beside, first, 1).start()
            w_direct(behind, 1 - first, 2).start()
    else:

        @pl.loop(1, n_chip)
        def _(step):
            for half in (0, 1):
                w_direct(lax.rem(chip + step, n_chip), half, step).start()

    own_w_across = [
        push(own_rows(half), w_at(c, half), w_fwd.at[0, half], w_recv.at[c, half], sibling, z)
        for half in (0, 1)
    ]
    for half in (0, 1):
        own_w_across[half].start()
        own_w[half].start()

    def w_pass(chip_from, half, slot):
        owner = chip_from * CORES + core
        w_arrival(owner, half).wait_recv()
        w_across(owner, half, slot).start()

    @pl.loop(0, n_chip)
    def _(step):
        for part in (0, 1):
            kv_arrival(sibling_source(step), part).wait_recv()

    def z_copy(owner, block, sems, to_z):
        rows = att_buf.at[owner, pl.ds(pl.multiple_of(block * BLK, BLK), BLK)]
        return push(rows, rows, sems.at[owner, block], z_recv.at[owner, block], c, to_z)

    exponent_scale = math.log2(math.e) / math.sqrt(head_size)

    @pl.loop(0, blocks)
    def _(block):
        place = c * blocks + block
        picks = [place] + [jnp.maximum(place - slash_ref[0, j], 0) for j in range(n_slash)]
        picks += [vert_ref[0, j] for j in range(n_vert)]
        picks += [place] * (n_slots - len(picks))
        for j, pick in enumerate(picks):
            kg[j * BLK:(j + 1) * BLK, :] = kv_buf[0, pick]
            vg[j * BLK:(j + 1) * BLK, :] = kv_buf[1, pick]

        first_row = pl.multiple_of(block * BLK, BLK)
        part = heads // 2
        for half in range(2):
            rows = q_buf[half * part:(half + 1) * part, pl.ds(first_row, BLK), :]
            scores = lax.dot_general(
                rows.reshape(part * BLK, head_size), kg[...], (((1,), (1,)), ((), ())),
                preferred_element_type=jnp.float32,
            )
            scores = scores.reshape(part, BLK, n_slots * BLK) + bias[block][None]
            scores = scores.reshape(part * BLK, n_slots * BLK)
            peak = jnp.max(scores, axis=-1, keepdims=True)
            weights = jnp.exp2((scores - peak) * exponent_scale)
            total = jnp.sum(weights, axis=-1, keepdims=True)
            mixed = jnp.dot(
                weights.astype(jnp.bfloat16), vg[...], preferred_element_type=jnp.float32
            )
            mixed = (mixed / total).astype(jnp.bfloat16)
            for h in range(part):
                col = (half * part + h) * head_size
                att_buf[z, pl.ds(first_row, BLK), col:col + head_size] = mixed[
                    h * BLK:(h + 1) * BLK
                ]

        @pl.when(z < n_kvh - 1)
        def _():
            z_copy(z, block, z_up, z + 1).start()

        @pl.when(z > 0)
        def _():
            z_copy(z, block, z_down, z - 1).start()

    def line_step(block, distance):
        @pl.when(z >= distance)
        def _():
            z_copy(z - distance, block, z_up, z).wait_recv()

            if distance < n_kvh - 1:
                @pl.when(z < n_kvh - 1)
                def _():
                    z_copy(z - distance, block, z_up, z + 1).start()

        @pl.when(z + distance < n_kvh)
        def _():
            z_copy(z + distance, block, z_down, z).wait_recv()

            if distance < n_kvh - 1:
                @pl.when(z > 0)
                def _():
                    z_copy(z + distance, block, z_down, z - 1).start()

    if square:
        for half, chip_from, slot in ((0, beside, 1), (1, behind, 2)):
            w_arrival(chip_from * CORES + core, half).wait_recv()
            w_corner(half).start()
            w_across(chip_from * CORES + core, half, slot).start()

    for distance in range(1, n_kvh - 1):

        @pl.loop(0, blocks)
        def _(block, distance=distance):
            line_step(block, distance)

        if square and distance == 1:
            w_pass(beside, 1, 1)
            w_pass(behind, 0, 2)

    if square:
        for half in (0, 1):
            w_pass(corner, half, 3)
    else:

        @pl.loop(1, n_chip)
        def _(step):
            for half in (0, 1):
                w_pass(lax.rem(chip + step, n_chip), half, step)

    @pl.loop(0, n_chip)
    def _(step):
        for half in (0, 1):
            w_arrival(sibling_source(step), half).wait_recv()

    for half in (0, 1):
        own_w[half].wait()

    depth = att_buf.shape[2]
    tile = 256
    n_tiles = out_ref.shape[1] // tile
    parts = 2
    part_rows = tokens // parts
    part_blocks = blocks // parts

    def out_copy(p):
        rows = pl.ds(pl.multiple_of(p * part_rows, part_rows), part_rows)
        return pltpu.make_async_copy(out_buf.at[rows], out_ref.at[rows], out_sem.at[p])

    def product(owner, rows, cols):
        return jnp.dot(
            att_buf[owner, rows, :],
            w_buf[pl.ds(pl.multiple_of(owner * depth, depth), depth), cols],
            preferred_element_type=jnp.float32,
        )

    def add_product(owner):
        @pl.loop(0, n_tiles)
        def _(j):
            cols = pl.ds(pl.multiple_of(j * tile, tile), tile)
            acc[:, cols] += product(owner, slice(None), cols)

    @pl.loop(0, n_tiles)
    def _(j):
        cols = pl.ds(pl.multiple_of(j * tile, tile), tile)
        acc[:, cols] = product(z, slice(None), cols)

    for distance in range(1, n_kvh - 1):

        @pl.when(z >= distance)
        def _(distance=distance):
            add_product(z - distance)

        @pl.when(z + distance < n_kvh)
        def _(distance=distance):
            add_product(z + distance)

    last = n_kvh - 1
    at_end = (z == 0) | (z == last)
    far = last - z

    @pl.when(at_end)
    def _():
        @pl.loop(0, parts)
        def _(p):
            @pl.loop(0, part_blocks)
            def _(b):
                line_step(p * part_blocks + b, last)

            rows = pl.ds(pl.multiple_of(p * part_rows, part_rows), part_rows)

            @pl.loop(0, n_tiles)
            def _(j):
                cols = pl.ds(pl.multiple_of(j * tile, tile), tile)
                total = acc[rows, cols] + product(far, rows, cols)
                out_buf[rows, cols] = total.astype(out_ref.dtype)

            out_copy(p).start()

    @pl.when(jnp.logical_not(at_end))
    def _():
        out_buf[...] = acc[...].astype(out_ref.dtype)

        @pl.loop(0, parts)
        def _(p):
            out_copy(p).start()

    @pl.loop(0, parts)
    def _(p):
        out_copy(p).wait()

    for part in (0, 1):
        own_across[part].wait_send()
    for half in (0, 1):
        own_w_across[half].wait_send()

    @pl.loop(1, n_chip)
    def _(step):
        for part in (0, 1):
            kv_across(c, part, step).wait_send()
        for half in (0, 1):
            w_across(c, half, step).wait_send()

    if square:
        for half in (0, 1):
            w_corner(half).wait_send()
            w_direct(beside, half, 1).wait_send()
            w_direct(behind, half, 2).wait_send()
            kv_corner(half).wait_send()
            kv_direct(beside, half, 1).wait_send()
            kv_direct(behind, half, 2).wait_send()
    else:

        @pl.loop(1, n_chip)
        def _(step):
            for half in (0, 1):
                w_direct(lax.rem(chip + step, n_chip), half, step).wait_send()
                kv_direct(lax.rem(chip + step, n_chip), half, step).wait_send()

    for distance in range(n_kvh):

        @pl.loop(0, blocks)
        def _(block, distance=distance):
            @pl.when((z >= distance) & (z < n_kvh - 1))
            def _():
                z_copy(z - distance, block, z_up, z + 1).wait_send()

            @pl.when((z + distance < n_kvh) & (z > 0))
            def _():
                z_copy(z + distance, block, z_down, z - 1).wait_send()


def line_kernel(
    n_ctx, n_kvh, n_slash, n_vert,
    vert_ref, slash_ref, q_ref, k_ref, v_ref, w_ref, out_ref,
    kv_buf, w_buf, att_buf, kg, vg, bias, q_raw, q_wide, q_buf, acc,
    mate_kv, mate_raw, mate_q, allow_out, allow_in, mate_bias,
    local_sem, kv_recv, kv_send, kv_fwd, w_recv, w_send, w_fwd, z_recv, z_up, z_down,
    mate_recv, mate_send, mkv_recv, mkv_send, mkv_fwd,
):
    c = lax.axis_index("ctx")
    z = lax.axis_index("kvh")
    n_chip = n_ctx // CORES
    chip, core = c // CORES, c % CORES
    sibling = chip * CORES + (1 - core)
    blocks = k_ref.shape[0]
    tokens, heads, head_size = q_ref.shape
    kv_refs = (k_ref, v_ref)
    w_rows = w_ref.shape[0]
    n_slots = kg.shape[0] // BLK

    def peer(step):
        return lax.rem(chip + step, n_chip) * CORES + core

    def sibling_source(step):
        return lax.rem(chip + n_chip - step, n_chip) * CORES + (1 - core)

    def kv_at(part, owner):
        return kv_buf.at[part, pl.ds(owner * blocks, blocks)]

    half_rows = w_rows // 2

    def w_at(owner, half):
        first = pl.multiple_of(owner * w_rows + half * half_rows, half_rows)
        return w_buf.at[pl.ds(first, half_rows)]

    def own_rows(half):
        return w_ref.at[pl.ds(half * half_rows, half_rows)]

    def push(src, dst, send_sem, recv_sem, to_ctx, to_z):
        return pltpu.make_async_remote_copy(
            src_ref=src, dst_ref=dst, send_sem=send_sem, recv_sem=recv_sem,
            device_id=(to_ctx, to_z), device_id_type=pl.DeviceIdType.MESH,
        )

    own_q = pltpu.make_async_copy(q_ref, q_raw, local_sem.at[2])
    own_q.start()
    own_w = [
        pltpu.make_async_copy(own_rows(half), w_at(c, half), local_sem.at[3 + half])
        for half in (0, 1)
    ]

    barrier = pltpu.get_barrier_semaphore()

    def greet(to_ctx, to_z):
        pl.semaphore_signal(
            barrier, inc=1, device_id=(to_ctx, to_z), device_id_type=pl.DeviceIdType.MESH
        )

    @pl.loop(1, n_chip)
    def _(step):
        greet(peer(step), z)

    greet(sibling, z)

    @pl.when(z > 0)
    def _():
        greet(c, z - 1)

    @pl.when(z < n_kvh - 1)
    def _():
        greet(c, z + 1)

    last = n_kvh - 1
    at_end = (z == 0) | (z == last)
    in_middle = jnp.logical_not(at_end)
    mate = z + 1 - 2 * (z % 2)
    first_again = blocks - AGAIN

    inner = jnp.where(z > 0, 1, 0) + jnp.where(z < n_kvh - 1, 1, 0)
    lane = lax.broadcasted_iota(jnp.int32, (BLK, 2 * BLK), 1)
    row = lax.broadcasted_iota(jnp.int32, (BLK, 2 * BLK), 0)

    key_block = lax.broadcasted_iota(jnp.int32, (8, 2 * BLK), 1)
    again_place = c * blocks + first_again + lax.broadcasted_iota(jnp.int32, (8, 2 * BLK), 0)
    kept = key_block == again_place
    for j in range(n_slash):
        kept = kept | (again_place - key_block == slash_ref[0, j])
    for j in range(n_vert):
        kept = kept | ((key_block == vert_ref[0, j]) & (key_block < again_place))
    allow_out[...] = jnp.where(kept, 1.0, 0.0)

    pl.semaphore_wait(barrier, n_chip + inner)

    square = n_chip == 4
    beside = (chip // 2) * 2 + (1 - chip % 2)
    behind = (1 - chip // 2) * 2 + chip % 2
    corner = n_chip - 1 - chip

    mate_pairs = (
        (k_ref, mate_kv.at[0, pl.ds(c * blocks, blocks)]),
        (v_ref, mate_kv.at[1, pl.ds(c * blocks, blocks)]),
        (allow_out, allow_in),
        (q_ref.at[pl.ds(first_again * BLK, AGAIN * BLK)], mate_raw),
    )

    def mate_copy(i):
        src, dst = mate_pairs[i]
        return push(src, dst, mate_send.at[i], mate_recv.at[i], c, mate)

    @pl.when(in_middle)
    def _():
        for i in range(len(mate_pairs)):
            mate_copy(i).start()

    own_kv = [
        pltpu.make_async_copy(kv_refs[part], kv_at(part, c), local_sem.at[part]) for part in (0, 1)
    ]

    def kv_direct(to_chip, part, slot):
        return push(
            kv_refs[part], kv_at(part, c), kv_send.at[part, slot], kv_recv.at[part, c],
            to_chip * CORES + core, z,
        )

    def kv_arrival(owner, part):
        rows = kv_at(part, owner)
        return push(rows, rows, kv_send.at[part, 0], kv_recv.at[part, owner], c, z)

    def kv_across(owner, part, slot):
        rows = kv_at(part, owner)
        return push(rows, rows, kv_fwd.at[part, slot], kv_recv.at[part, owner], sibling, z)

    def kv_corner(part):
        from_chip, to_chip = (beside, behind) if part == 0 else (behind, beside)
        owner = from_chip * CORES + core
        rows = kv_at(part, owner)
        return push(
            rows, rows, kv_send.at[part, 0], kv_recv.at[part, owner], to_chip * CORES + core, z
        )

    def kv_pass(chip_from, part, slot):
        owner = chip_from * CORES + core
        kv_arrival(owner, part).wait_recv()
        kv_across(owner, part, slot).start()

    own_across = [
        push(kv_refs[part], kv_at(part, c), kv_fwd.at[part, 0], kv_recv.at[part, c], sibling, z)
        for part in (0, 1)
    ]

    if square:
        for first in (0, 1):
            kv_direct(beside, first, 1).start()
            kv_direct(behind, 1 - first, 2).start()
    else:

        @pl.loop(1, n_chip)
        def _(step):
            for part in (0, 1):
                kv_direct(lax.rem(chip + step, n_chip), part, step).start()

    for part in (0, 1):
        own_across[part].start()
        own_kv[part].start()

    @pl.loop(0, blocks)
    def _(block):
        place = c * blocks + block
        fills = [jnp.float32(0.0)]
        for j in range(n_slash):
            fills.append(jnp.where(place - slash_ref[0, j] >= 0, 0.0, NEG_FILL))
        for j in range(n_vert):
            gap = place - vert_ref[0, j]
            fill = jnp.where(gap > 0, 0.0, NEG_FILL)
            for k in range(n_slash):
                fill = jnp.where(gap == slash_ref[0, k], NEG_FILL, fill)
            fills.append(fill)
        while len(fills) < n_slots:
            fills.append(jnp.float32(NEG_FILL))
        for j in range(0, n_slots, 2):
            fill = jnp.where(lane < BLK, fills[j], fills[j + 1])
            if j == 0:
                fill = jnp.where((lane < BLK) & (lane > row), NEG_FILL, fill)
            bias[block, :, j * BLK:(j + 2) * BLK] = fill

    for part in (0, 1):
        own_kv[part].wait()

    if square:
        for part, chip_from, slot in ((0, beside, 1), (1, behind, 2)):
            kv_arrival(chip_from * CORES + core, part).wait_recv()
            kv_corner(part).start()
            kv_across(chip_from * CORES + core, part, slot).start()

    own_q.wait()

    @pl.loop(0, blocks)
    def _(block):
        first_row = pl.multiple_of(block * BLK, BLK)
        wide = q_raw[pl.ds(first_row, BLK)].astype(jnp.float32)
        q_wide[...] = wide.reshape(BLK * heads, head_size)
        for h in range(heads):
            q_buf[h, pl.ds(first_row, BLK), :] = q_wide[
                pl.ds(h, BLK, stride=heads), :
            ].astype(jnp.bfloat16)

    if square:
        kv_pass(beside, 1, 1)
        kv_pass(behind, 0, 2)
        for part in (0, 1):
            kv_pass(corner, part, 3)
    else:

        @pl.loop(1, n_chip)
        def _(step):
            for part in (0, 1):
                kv_pass(lax.rem(chip + step, n_chip), part, step)

    def mkv_at(part, chip_of, core_of):
        return mate_kv.at[part, pl.ds((chip_of * CORES + core_of) * blocks, blocks)]

    def mkv_copy(chip_of, part, sem, to_ctx):
        rows = mkv_at(part, chip_of, core)
        return push(rows, rows, sem, mkv_recv.at[part, chip_of * CORES + core], to_ctx, z)

    def mkv_direct(to_chip, part, slot):
        return mkv_copy(chip, part, mkv_send.at[part, slot], to_chip * CORES + core)

    def mkv_across(chip_of, part, slot):
        return mkv_copy(chip_of, part, mkv_fwd.at[part, slot], sibling)

    def mkv_corner(part):
        from_chip, to_chip = (beside, behind) if part == 0 else (behind, beside)
        return mkv_copy(from_chip, part, mkv_send.at[part, 0], to_chip * CORES + core)

    def mkv_arrival(chip_of, core_of, part):
        rows = mkv_at(part, chip_of, core_of)
        return push(
            rows, rows, mkv_send.at[part, 0], mkv_recv.at[part, chip_of * CORES + core_of],
            sibling, z,
        )

    @pl.when(at_end)
    def _():
        for i in (0, 1):
            mate_copy(i).wait_recv()
        for first in (0, 1):
            mkv_direct(beside, first, 1).start()
            mkv_direct(behind, 1 - first, 2).start()
        for part in (0, 1):
            mkv_across(chip, part, 0).start()

    def w_direct(to_chip, half, slot):
        return push(
            own_rows(half), w_at(c, half), w_send.at[slot, half], w_recv.at[c, half],
            to_chip * CORES + core, z,
        )

    def w_arrival(owner, half):
        return push(
            w_at(owner, half), w_at(owner, half), w_send.at[0, half], w_recv.at[owner, half], c, z
        )

    def w_across(owner, half, slot):
        return push(
            w_at(owner, half), w_at(owner, half), w_fwd.at[slot, half], w_recv.at[owner, half],
            sibling, z,
        )

    def w_corner(half):
        from_chip, to_chip = (beside, behind) if half == 0 else (behind, beside)
        owner = from_chip * CORES + core
        return push(
            w_at(owner, half), w_at(owner, half), w_send.at[0, half], w_recv.at[owner, half],
            to_chip * CORES + core, z,
        )

    w_direct(beside, 0, 1).start()
    w_direct(behind, 1, 2).start()

    own_w_across = [
        push(own_rows(half), w_at(c, half), w_fwd.at[0, half], w_recv.at[c, half], sibling, z)
        for half in (0, 1)
    ]
    for half in (0, 1):
        own_w_across[half].start()
        own_w[half].start()

    def w_pass(chip_from, half, slot):
        owner = chip_from * CORES + core
        w_arrival(owner, half).wait_recv()
        w_across(owner, half, slot).start()

    @pl.loop(0, n_chip)
    def _(step):
        for part in (0, 1):
            kv_arrival(sibling_source(step), part).wait_recv()

    def z_copy(owner, block, sems, to_z):
        rows = att_buf.at[owner, pl.ds(pl.multiple_of(block * BLK, BLK), BLK)]
        return push(rows, rows, sems.at[owner, block], z_recv.at[owner, block], c, to_z)

    def sent(block, owner, to_z):
        ends = ((owner == 1) & (to_z == 0)) | ((owner == last - 1) & (to_z == last))
        return jnp.logical_not(ends & (block >= first_again))

    def line_step(block, distance):
        @pl.when((z >= distance) & sent(block, z - distance, z))
        def _():
            z_copy(z - distance, block, z_up, z).wait_recv()

            if distance < n_kvh - 1:
                @pl.when(z < n_kvh - 1)
                def _():
                    z_copy(z - distance, block, z_up, z + 1).start()

        @pl.when((z + distance < n_kvh) & sent(block, z + distance, z))
        def _():
            z_copy(z + distance, block, z_down, z).wait_recv()

            if distance < n_kvh - 1:
                @pl.when(z > 0)
                def _():
                    z_copy(z + distance, block, z_down, z - 1).start()

    exponent_scale = math.log2(math.e) / math.sqrt(head_size)

    @pl.loop(0, blocks)
    def _(block):
        place = c * blocks + block
        picks = [place] + [jnp.maximum(place - slash_ref[0, j], 0) for j in range(n_slash)]
        picks += [vert_ref[0, j] for j in range(n_vert)]
        picks += [place] * (n_slots - len(picks))
        for j, pick in enumerate(picks):
            kg[j * BLK:(j + 1) * BLK, :] = kv_buf[0, pick]
            vg[j * BLK:(j + 1) * BLK, :] = kv_buf[1, pick]

        first_row = pl.multiple_of(block * BLK, BLK)
        part = heads // 2
        for half in range(2):
            rows = q_buf[half * part:(half + 1) * part, pl.ds(first_row, BLK), :]
            scores = lax.dot_general(
                rows.reshape(part * BLK, head_size), kg[...], (((1,), (1,)), ((), ())),
                preferred_element_type=jnp.float32,
            )
            scores = scores.reshape(part, BLK, n_slots * BLK) + bias[block][None]
            scores = scores.reshape(part * BLK, n_slots * BLK)
            peak = jnp.max(scores, axis=-1, keepdims=True)
            weights = jnp.exp2((scores - peak) * exponent_scale)
            total = jnp.sum(weights, axis=-1, keepdims=True)
            mixed = jnp.dot(
                weights.astype(jnp.bfloat16), vg[...], preferred_element_type=jnp.float32
            )
            mixed = (mixed / total).astype(jnp.bfloat16)
            for h in range(part):
                col = (half * part + h) * head_size
                att_buf[z, pl.ds(first_row, BLK), col:col + head_size] = mixed[
                    h * BLK:(h + 1) * BLK
                ]

        @pl.when((z < n_kvh - 1) & sent(block, z, z + 1))
        def _():
            z_copy(z, block, z_up, z + 1).start()

        @pl.when((z > 0) & sent(block, z, z - 1))
        def _():
            z_copy(z, block, z_down, z - 1).start()

        @pl.when(block == 2)
        def _():
            @pl.when(at_end)
            def _():
                for part, chip_from, slot in ((0, beside, 1), (1, behind, 2)):
                    mkv_arrival(chip_from, core, part).wait_recv()
                    mkv_corner(part).start()
                    mkv_across(chip_from, part, slot).start()

            w_direct(beside, 1, 1).start()
            w_direct(behind, 0, 2).start()

        @pl.when(in_middle & (block >= EARLY))
        def _():
            line_step(block - EARLY, 1)

    for half, chip_from, slot in ((0, beside, 1), (1, behind, 2)):
        w_arrival(chip_from * CORES + core, half).wait_recv()
        w_corner(half).start()
        w_across(chip_from * CORES + core, half, slot).start()

    acc[...] = jnp.zeros_like(acc)

    @pl.when(in_middle)
    def _():
        @pl.loop(blocks - EARLY, min(EARLY + 1, blocks))
        def _(block):
            line_step(block, 1)

        @pl.loop(0, max(blocks - 1 - EARLY, 0))
        def _(block):
            line_step(block, 2)
            line_step(EARLY + 1 + block, 1)

    @pl.when(at_end)
    def _():
        mkv_pass = ((beside, 1, 1), (behind, 0, 2), (corner, 0, 3), (corner, 1, 3))
        for chip_from, part, slot in mkv_pass:
            mkv_arrival(chip_from, core, part).wait_recv()
            mkv_across(chip_from, part, slot).start()
        for i in (2, 3):
            mate_copy(i).wait_recv()

        @pl.loop(0, n_chip)
        def _(chip_of):
            for part in (0, 1):
                mkv_arrival(chip_of, 1 - core, part).wait_recv()

        @pl.loop(0, AGAIN)
        def _(b):
            first_row = pl.multiple_of(b * BLK, BLK)
            wide = mate_raw[pl.ds(first_row, BLK)].astype(jnp.float32)
            q_wide[...] = wide.reshape(BLK * heads, head_size)
            for h in range(heads):
                mate_q[h, pl.ds(first_row, BLK), :] = q_wide[
                    pl.ds(h, BLK, stride=heads), :
                ].astype(jnp.bfloat16)

        keys = n_ctx * blocks * BLK
        spread = (
            lax.broadcasted_iota(jnp.int32, (2 * BLK, keys), 1) // BLK
            == lax.broadcasted_iota(jnp.int32, (2 * BLK, keys), 0)
        )
        allowed = jnp.dot(
            allow_in[...].astype(jnp.bfloat16),
            jnp.where(spread, 1.0, 0.0).astype(jnp.bfloat16),
            preferred_element_type=jnp.float32,
        )
        key_at = lax.broadcasted_iota(jnp.int32, (BLK, keys), 1)
        query_row = lax.broadcasted_iota(jnp.int32, (BLK, keys), 0)
        for b in range(AGAIN):
            query_at = (c * blocks + first_again + b) * BLK + query_row
            mate_bias[b] = jnp.where(
                (allowed[b:b + 1] > 0.5) & (key_at <= query_at), 0.0, NEG_FILL
            )

        @pl.loop(0, AGAIN * 4)
        def _(i):
            b, quarter = i // 4, i % 4
            part = heads // 4
            from_row = pl.multiple_of(b * BLK, BLK)
            rows = mate_q[pl.ds(quarter * part, part), pl.ds(from_row, BLK), :]
            scores = lax.dot_general(
                rows.reshape(part * BLK, head_size), mate_kv[0].reshape(keys, head_size),
                (((1,), (1,)), ((), ())), preferred_element_type=jnp.float32,
            )
            scores = scores.reshape(part, BLK, keys) + mate_bias[b][None]
            scores = scores.reshape(part * BLK, keys)
            peak = jnp.max(scores, axis=-1, keepdims=True)
            weights = jnp.exp2((scores - peak) * exponent_scale)
            total = jnp.sum(weights, axis=-1, keepdims=True)
            mixed = jnp.dot(
                weights.astype(jnp.bfloat16), mate_kv[1].reshape(keys, head_size),
                preferred_element_type=jnp.float32,
            )
            mixed = (mixed / total).astype(jnp.bfloat16)
            to_row = pl.multiple_of((first_again + b) * BLK, BLK)
            for h in range(part):
                col = pl.multiple_of((quarter * part + h) * head_size, head_size)
                att_buf[mate, pl.ds(to_row, BLK), pl.ds(col, head_size)] = mixed[
                    h * BLK:(h + 1) * BLK
                ]

    depth = att_buf.shape[2]
    tile = 256
    n_tiles = out_ref.shape[1] // tile
    parts = OUT_PARTS
    part_rows = tokens // parts
    part_blocks = blocks // parts

    def product(owner, rows, cols):
        return jnp.dot(
            att_buf[owner, rows, :],
            w_buf[pl.ds(pl.multiple_of(owner * depth, depth), depth), cols],
            preferred_element_type=jnp.float32,
        )

    def add_product(owner):
        @pl.loop(0, n_tiles)
        def _(j):
            cols = pl.ds(pl.multiple_of(j * tile, tile), tile)
            acc[:, cols] += product(owner, slice(None), cols)

    far = last - z

    def add_in_full(chip_of):
        @pl.when(jnp.logical_not(at_end & (chip_of == far)))
        def _():
            add_product(chip_of)

    def w_ready(chip_of):
        for half in (0, 1):
            w_arrival(chip_of * CORES + (1 - core), half).wait_recv()

    w_pass(beside, 1, 1)
    w_pass(behind, 0, 2)

    @pl.when(in_middle)
    def _():
        @pl.loop(max(blocks - 1 - EARLY, 0), blocks)
        def _(block):
            line_step(block, 2)

    @pl.when(at_end)
    def _():
        for distance in (1, 2):

            @pl.loop(0, blocks)
            def _(block, distance=distance):
                line_step(block, distance)

    for half in (0, 1):
        own_w[half].wait()
    for chip_of in (chip, beside, behind):
        w_ready(chip_of)
        add_in_full(chip_of)

    for half in (0, 1):
        w_pass(corner, half, 3)
    w_ready(corner)
    add_in_full(corner)

    @pl.when(in_middle)
    def _():
        out_ref[...] = acc[...].astype(out_ref.dtype)

    for part in (0, 1):
        own_across[part].wait_send()
    for half in (0, 1):
        own_w_across[half].wait_send()

    @pl.loop(1, n_chip)
    def _(step):
        for part in (0, 1):
            kv_across(c, part, step).wait_send()
        for half in (0, 1):
            w_across(c, half, step).wait_send()

    if square:
        for half in (0, 1):
            w_corner(half).wait_send()
            w_direct(beside, half, 1).wait_send()
            w_direct(behind, half, 2).wait_send()
            kv_corner(half).wait_send()
            kv_direct(beside, half, 1).wait_send()
            kv_direct(behind, half, 2).wait_send()
    else:

        @pl.loop(1, n_chip)
        def _(step):
            for half in (0, 1):
                w_direct(lax.rem(chip + step, n_chip), half, step).wait_send()
                kv_direct(lax.rem(chip + step, n_chip), half, step).wait_send()

    for distance in range(n_kvh):

        @pl.loop(0, blocks)
        def _(block, distance=distance):
            @pl.when((z >= distance) & (z < n_kvh - 1) & sent(block, z - distance, z + 1))
            def _():
                z_copy(z - distance, block, z_up, z + 1).wait_send()

            @pl.when((z + distance < n_kvh) & (z > 0) & sent(block, z + distance, z - 1))
            def _():
                z_copy(z + distance, block, z_down, z - 1).wait_send()

    @pl.when(in_middle)
    def _():
        for i in range(len(mate_pairs)):
            mate_copy(i).wait_send()

    @pl.when(at_end)
    def _():
        for part in (0, 1):
            mkv_corner(part).wait_send()
            mkv_direct(beside, part, 1).wait_send()
            mkv_direct(behind, part, 2).wait_send()
            for slot in range(n_chip):
                mkv_across(chip, part, slot).wait_send()

    @pl.when(at_end)
    def _():
        @pl.loop(0, parts)
        def _(p):
            @pl.loop(0, part_blocks)
            def _(b):
                line_step(p * part_blocks + b, last)

            rows = pl.ds(pl.multiple_of(p * part_rows, part_rows), part_rows)

            @pl.loop(0, n_tiles, unroll=True)
            def _(j):
                cols = pl.ds(pl.multiple_of(j * tile, tile), tile)
                total = acc[rows, cols] + product(far, rows, cols)
                out_ref[rows, cols] = total.astype(out_ref.dtype)


def solution(mesh):
    n_ctx, n_kvh = mesh.shape["ctx"], mesh.shape["kvh"]

    def on_device(queries, keys, values, vert_blocks, slash_offsets, out_weight):
        tokens, heads, head_size = queries.shape
        blocks = tokens // BLK
        n_slash, n_vert = slash_offsets.shape[1], vert_blocks.shape[1]
        n_slots = 1 + n_slash + n_vert
        n_slots += n_slots % 2
        w_rows, _, w_cols = out_weight.shape
        n_chip = n_ctx // CORES
        k = keys.reshape(blocks, BLK, head_size)
        v = values.reshape(blocks, BLK, head_size)
        dma = pltpu.SemaphoreType.DMA
        shared = [
            pltpu.VMEM((n_slots * BLK, head_size), jnp.bfloat16),
            pltpu.VMEM((n_slots * BLK, head_size), jnp.bfloat16),
            pltpu.VMEM((blocks, BLK, n_slots * BLK), jnp.float32),
            pltpu.VMEM((tokens, heads, head_size), jnp.bfloat16),
            pltpu.VMEM((BLK * heads, head_size), jnp.float32),
            pltpu.VMEM((heads, tokens, head_size), jnp.bfloat16),
        ]
        kv_buf = pltpu.VMEM((2, n_ctx * blocks, BLK, head_size), jnp.bfloat16)
        scratch = [
            kv_buf,
            pltpu.VMEM((n_ctx * w_rows, w_cols), jnp.bfloat16),
            pltpu.VMEM((n_kvh, tokens, heads * head_size), jnp.bfloat16),
            *shared,
            pltpu.VMEM((tokens, w_cols), jnp.float32),
        ]
        sems = [
            dma((5,)),
            dma((2, n_ctx)),
            dma((2, n_chip)),
            dma((2, n_chip)),
            dma((n_ctx, 2)),
            dma((n_chip, 2)),
            dma((n_chip, 2)),
            dma((n_kvh, blocks)),
            dma((n_kvh, blocks)),
            dma((n_kvh, blocks)),
        ]
        if n_chip == 4 and n_kvh == 4 and n_ctx * blocks <= 2 * BLK:
            body = functools.partial(line_kernel, n_ctx, n_kvh, n_slash, n_vert)
            out_space, limit = pltpu.VMEM, 50 * 2**20
            scratch += [
                kv_buf,
                pltpu.VMEM((AGAIN * BLK, heads, head_size), jnp.bfloat16),
                pltpu.VMEM((heads, AGAIN * BLK, head_size), jnp.bfloat16),
                pltpu.VMEM((8, 2 * BLK), jnp.float32),
                pltpu.VMEM((8, 2 * BLK), jnp.float32),
                pltpu.VMEM((AGAIN, BLK, n_ctx * tokens), jnp.float32),
                *sems,
                dma((4,)),
                dma((4,)),
                dma((2, n_ctx)),
                dma((2, n_chip)),
                dma((2, n_chip)),
            ]
        else:
            body = functools.partial(kernel, n_ctx, n_kvh, n_slash, n_vert)
            out_space, limit = pl.ANY, 56 * 2**20
            scratch += [pltpu.VMEM((tokens, w_cols), jnp.bfloat16), *sems, dma((2,))]
        return pl.pallas_call(
            body,
            out_shape=jax.ShapeDtypeStruct((tokens, w_cols), jnp.bfloat16),
            in_specs=[
                pl.BlockSpec(memory_space=pltpu.SMEM),
                pl.BlockSpec(memory_space=pltpu.SMEM),
                pl.BlockSpec(memory_space=pl.ANY),
                pl.BlockSpec(memory_space=pl.ANY),
                pl.BlockSpec(memory_space=pl.ANY),
                pl.BlockSpec(memory_space=pl.ANY),
            ],
            out_specs=pl.BlockSpec(memory_space=out_space),
            scratch_shapes=scratch,
            compiler_params=pltpu.CompilerParams(
                collective_id=0, has_side_effects=True, vmem_limit_bytes=limit
            ),
        )(
            *(
                pltpu.with_memory_space_constraint(x, pltpu.HBM)
                for x in (vert_blocks, slash_offsets, queries, k, v, out_weight.reshape(w_rows, w_cols))
            ),
        )

    return jax.shard_map(
        on_device,
        mesh=mesh,
        in_specs=(
            P("ctx", "kvh", None),
            P("ctx", "kvh", None),
            P("ctx", "kvh", None),
            P("kvh", None),
            P("kvh", None),
            P("ctx", "kvh", None),
        ),
        out_specs=P("ctx", "kvh"),
        check_vma=False,
    )
```
